32 devices in a mesh: seq: 2 (over x), ep: 16 (over z, y, core).
Axes of the slice: x: 2, y: 2, z: 4, core: 2. Of those that a mesh axis runs over, the one named last changes fastest.
Arguments:
- tokens: bfloat16 [256, 7168], P(('seq', 'ep')), may hold values from -50 to 50
- out_grad: bfloat16 [256, 7168], P(('seq', 'ep')), may hold values from -6 to 6
- routes: int32 [256, 8], P(('seq', 'ep')), may hold values from 0 to 15, all different within a row; in each aligned block of 8 rows (0 to 7, 8 to 15, ...) at most 5 rows name the same one
- gate_fixed: int32 [256, 8], P(('seq', 'ep')), may hold values from 1 to 65535
- ramp_step: int32 [16], replicated, may hold values from 1 to 8
- norm_gain: float32 [7168], replicated, may hold values from 0.1 to 1.9
- w_gate: bfloat16 [16, 7168, 1024], P('ep', None, 'seq'), may hold values from -0.0625 to 0.0625
- w_up: bfloat16 [16, 7168, 1024], P('ep', None, 'seq'), may hold values from -0.0625 to 0.0625
- w_down: bfloat16 [16, 1024, 7168], P('ep', 'seq'), may hold values from -0.1875 to 0.1875
Outputs:
- mixed: bfloat16 [256, 7168], P(('seq', 'ep'))
- tokens_grad: bfloat16 [256, 7168], P(('seq', 'ep'))
- gain_grad: float32 [7168], P(('seq', 'ep'))
- w_gate_grad: bfloat16 [16, 7168, 1024], P('ep', None, 'seq')
- w_up_grad: bfloat16 [16, 7168, 1024], P('ep', None, 'seq')
- w_down_grad: bfloat16 [16, 1024, 7168], P('ep', 'seq')
The draws below stay inside these ranges and needn't reach their ends.
Inputs may be any that keep to these rules, and one draw needn't show every extreme that they name: `routes`: each row names 8 different experts. Within the rows of one device (aligned blocks of 8 rows) no expert is named more than 5 times, and in some such block one expert is named exactly 5 times.
All inputs are finite; a program needn't handle non-finite values.
Results may differ from the reference program's by a relative error of at most 0.023.
Values may be sent and summed in bfloat16 or wider, within the bound.
No kernel may reach another device: no remote copies, remote signals or barrier semaphores. Data moves between devices by JAX's collectives and lax.ppermute only.
A program may use at most 128 MiB of HBM per device.

```python
import math
import jax
import jax.numpy as jnp
import numpy as np
from jax import lax

D = 7168
FFW = 1024
TOP = 8
RAMP = 8
TOK_DEV = 8
EXPERTS = 16
CAP = 5
TOKENS = 256
N_SEQ = 2
N_EP = 16


def draw_tokens(key, part):
    key_base, key_column, key_row = jax.random.split(key, 3)
    column = jnp.exp(jax.random.uniform(key_column, (D,), jnp.float32, 0.0, math.log(10.0)))
    row_scale = jnp.exp(jax.random.uniform(key_row, (TOKENS, 1), jnp.float32, 0.0, math.log(10.0)))
    base = jax.random.normal(key_base, (TOKENS, D), jnp.float32)
    base = jnp.clip(base, -5.0, 5.0)
    return (base * column[None, :] * row_scale / 10.0).astype(jnp.bfloat16)


def draw_ramp_step(key, part):
    key_steps, key_order = jax.random.split(key, 2)
    steps = jax.random.randint(key_steps, (EXPERTS,), 1, RAMP + 1, jnp.int32)
    order = jax.random.permutation(key_order, EXPERTS)
    steps = steps.at[order[0]].set(RAMP)
    steps = steps.at[order[1]].set(1)
    return steps


def plant(drawn, rng, low, top_value):
    extent = drawn.shape
    spot = [jax.random.randint(jax.random.fold_in(rng, axis), (), 0, extent[axis]) for axis in range(len(extent))]
    drawn = drawn.at[tuple(spot)].set(low)
    longest = extent.index(max(extent))
    spot[longest] = (spot[longest] + 1) % extent[longest]
    return drawn.at[tuple(spot)].set(top_value)


def raised(array, own_key, source, target, shards_of, factor):
    owner, partner = [(jnp.arange(array.shape[dim]) // (array.shape[dim] // shards_of)).reshape([-1 if axis == dim else 1 for axis in range(array.ndim)]) for dim in (source, target)]
    chosen = jax.random.permutation(own_key, shards_of)[partner]
    strong = (owner == chosen) | (owner == (partner + shards_of // 2) % shards_of)
    return jnp.where(strong, factor * array, array)


def level_of(own_key, dims, shards, least, top_value):
    level, own = 1.0, jax.random.fold_in(own_key, 6)
    for axis_at, shards_of in shards:
        draws = jnp.exp(jax.random.uniform(jax.random.fold_in(own, axis_at), (shards_of,), jnp.float32, least / len(shards), top_value / len(shards)))
        level = level * jnp.repeat(draws, dims[axis_at] // shards_of).reshape([-1 if axis == axis_at else 1 for axis in range(len(dims))])
    return level


def deal_out(own_key, own, number, rows, amount, top, reach, lean):
    sequence = jax.random.permutation(own_key, amount)
    crowded, common = portions_of(amount, rows * top, reach, lean, True), portions_of(amount, rows * top, reach, lean, False)
    places = jnp.arange(amount)

    def named(sizes, offset_by):
        used = int((sizes > 0).sum())
        fixed = max(1, used // 4)
        shifted = fixed + (places - fixed + offset_by * (used - fixed)) % max(1, amount - fixed)
        return jnp.zeros((amount,), jnp.int32).at[sequence[jnp.where(places < fixed, places, shifted)]].set(jnp.asarray(sizes, jnp.int32))

    sizes = jnp.where(number % 4 == 0, named(crowded, number // 4), named(common, number - number // 4 - 1))
    mixed = jax.random.permutation(jax.random.fold_in(own, 3), amount)
    donor, receiver = mixed[0:amount // 2 * 2:2], mixed[1:amount // 2 * 2:2]
    slack = jnp.minimum(sizes[donor] - 1, reach - sizes[receiver]) // 2
    slack = jnp.where((donor == sequence[0]) | (receiver == sequence[0]) | (sizes[receiver] == 0), 0, jnp.maximum(slack, 0))
    shifted = jax.random.randint(jax.random.fold_in(own, 4), (amount // 2,), 0, 1 << 20) % (slack + 1)
    sizes = sizes.at[donor].add(-shifted).at[receiver].add(shifted)
    items = jnp.searchsorted(jnp.cumsum(sizes), jnp.arange(rows * top), side="right").astype(jnp.int32)
    listing = items.reshape(top, rows).T
    listing = listing[jax.random.permutation(jax.random.fold_in(own, 1), rows)]
    offset_by = jax.random.randint(jax.random.fold_in(own, 2), (rows, 1), 0, top)
    return jnp.take_along_axis(listing, (jnp.arange(top)[None, :] + offset_by) % top, axis=1)


def portions_of(count, total, bound, skew, full):
    loads = [(1 << 20) // math.isqrt(standing ** skew) + 1 for standing in range(1, count + 1)]
    largest = bound if full else min(bound, max(-(-total // count), total * loads[0] // sum(loads)))
    least = 1 if total - largest >= count - 1 else 0
    counts, spare = [largest] + [least] * (count - 1), total - largest - least * (count - 1)
    while spare > 0:
        movable = [i for i in range(1, count) if counts[i] < largest] or [i for i in range(1, count) if counts[i] < bound]
        mass, budget = sum([loads[i] for i in movable]), spare
        for i in movable:
            extra = min(bound - counts[i], max(1, budget * loads[i] // mass), spare)
            counts[i] = counts[i] + extra
            spare = spare - extra
    return np.array(counts)


def noise(stream_key, dims, width, limit, pieces=(), held_as=jnp.bfloat16):
    entries = width * jax.random.normal(stream_key, dims, jnp.float32)
    if pieces:
        entries = entries * level_of(stream_key, dims, pieces, -0.22, 0.18)
    return jnp.clip(entries, -limit, limit).astype(held_as)


def noise_with(own_key, shape, spread, limit, cuts, heavy, held_as=jnp.bfloat16):
    drawn = spread * jax.random.normal(own_key, shape, jnp.float32)
    if cuts:
        drawn = drawn * level_of(own_key, shape, cuts, -0.22, 0.18)
    return jnp.clip(raised(drawn, jax.random.fold_in(own_key, 3), *heavy), -limit, limit).astype(held_as)


def setup_inputs(seed: int = 0) -> dict:
    splits = jax.random.split(jax.random.key(seed), 10)
    tokens = draw_tokens(jax.random.fold_in(splits[9], 71), 0)
    out_grad = noise_with(splits[1], (TOKENS, D), 1.0, 6.0, ((0, 32),), (0, 1, 32, 2.75))
    routes_keys = jax.random.split(jax.random.fold_in(splits[2], 1), TOKENS // TOK_DEV)
    routes_turns = jax.random.permutation(jax.random.fold_in(splits[2], 3), TOKENS // TOK_DEV)
    routes = jax.vmap(lambda own, number: deal_out(jax.random.fold_in(splits[2], 2), own, number, TOK_DEV, EXPERTS, TOP, CAP, 2))(routes_keys, routes_turns).reshape((TOKENS, TOP))
    gate_fixed = plant(jax.random.randint(splits[3], (TOKENS, TOP), 1, 65536), jax.random.fold_in(splits[3], 1), 1, 65535).astype(jnp.int32)
    ramp_step = draw_ramp_step(jax.random.fold_in(splits[9], 71), 0)
    norm_gain = jnp.clip(1.0 + 0.18 * jax.random.normal(splits[5], (D,), jnp.float32), 0.1, 1.9)
    w_gate = noise(splits[6], (EXPERTS, D, FFW), D ** -0.5, 0.0625, ((0, 16), (2, 2)))
    w_up = noise(splits[7], (EXPERTS, D, FFW), D ** -0.5, 0.0625, ((0, 16), (2, 2)))
    w_down = noise(splits[8], (EXPERTS, FFW, D), FFW ** -0.5, 0.1875, ((0, 16), (1, 2)))
    return {"tokens": tokens, "out_grad": out_grad, "routes": routes, "gate_fixed": gate_fixed, "ramp_step": ramp_step, "norm_gain": norm_gain, "w_gate": w_gate, "w_up": w_up, "w_down": w_down}


gate_unit = 65536.0
norm_eps = 1e-06

def reference(tokens, out_grad, routes, gate_fixed, ramp_step, norm_gain, w_gate, w_up, w_down):
    blocks = N_SEQ * N_EP
    per_expert = blocks * CAP
    quarter = FFW // N_SEQ
    tokens_wide = tokens.astype(jnp.float32)
    recip = lax.rsqrt(lax.optimization_barrier(jnp.mean(tokens_wide * tokens_wide, axis=1, keepdims=True)) + norm_eps)
    normed = (tokens_wide * recip * norm_gain[None, :]).astype(jnp.bfloat16)
    flat = routes.reshape(blocks, TOK_DEV * TOP)
    onehot = (flat[:, :, None] == jnp.arange(EXPERTS, dtype=jnp.int32)[None, None, :]).astype(jnp.int32)
    position = lax.optimization_barrier(jnp.sum(jnp.cumsum(onehot, axis=1) * onehot, axis=2)) - 1
    block_ids = jnp.arange(blocks, dtype=jnp.int32)[:, None]
    flat_index = (flat * per_expert + block_ids * CAP + position).reshape(-1).astype(jnp.int32)
    pair_ids = jnp.arange(TOKENS * TOP, dtype=jnp.int32)
    table = jnp.full((EXPERTS * per_expert,), TOKENS * TOP, jnp.int32).at[flat_index].set(pair_ids)
    ramp_pick = ramp_step[routes.reshape(-1)].astype(jnp.float32)
    coef = gate_fixed.reshape(-1).astype(jnp.float32) / gate_unit * ramp_pick / RAMP
    grad_rows = (coef[:, None] * jnp.repeat(out_grad.astype(jnp.float32), TOP, axis=0)).astype(jnp.bfloat16)
    normed_pad = jnp.concatenate([normed, jnp.zeros((1, D), jnp.bfloat16)], axis=0)
    grad_pad = jnp.concatenate([grad_rows, jnp.zeros((1, D), jnp.bfloat16)], axis=0)

    def per_item(item):
        pair_rows, weight_gate, weight_up, weight_down = item
        rows_normed = normed_pad[pair_rows // TOP]
        rows_grad = grad_pad[pair_rows]
        pre_gate = jnp.dot(rows_normed, weight_gate, preferred_element_type=jnp.float32)
        pre_up = jnp.dot(rows_normed, weight_up, preferred_element_type=jnp.float32)
        sigma = jax.nn.sigmoid(pre_gate)
        active = pre_gate * sigma
        hidden = (active * pre_up).astype(jnp.bfloat16)
        hidden_q = hidden.astype(jnp.float32).reshape(per_expert, N_SEQ, quarter)
        down_q = weight_down.astype(jnp.float32).reshape(N_SEQ, quarter, D)
        parts = jnp.einsum('rqf,qfd->qrd', hidden_q, down_q).astype(jnp.bfloat16)
        slot_out = lax.optimization_barrier(jnp.sum(parts.astype(jnp.float32), axis=0)).astype(jnp.bfloat16)
        hidden_grad = jnp.dot(rows_grad, weight_down.T, preferred_element_type=jnp.float32)
        gate_pre_grad = (hidden_grad * pre_up * sigma * (1.0 + pre_gate * (1.0 - sigma))).astype(jnp.bfloat16)
        up_pre_grad = (hidden_grad * active).astype(jnp.bfloat16)
        down_grad = jnp.dot(hidden.T, rows_grad, preferred_element_type=jnp.float32).astype(jnp.bfloat16)
        gate_grad = jnp.dot(rows_normed.T, gate_pre_grad, preferred_element_type=jnp.float32).astype(jnp.bfloat16)
        up_grad = jnp.dot(rows_normed.T, up_pre_grad, preferred_element_type=jnp.float32).astype(jnp.bfloat16)
        gate_q = gate_pre_grad.astype(jnp.float32).reshape(per_expert, N_SEQ, quarter)
        up_q = up_pre_grad.astype(jnp.float32).reshape(per_expert, N_SEQ, quarter)
        wg_q = weight_gate.astype(jnp.float32).reshape(D, N_SEQ, quarter)
        wu_q = weight_up.astype(jnp.float32).reshape(D, N_SEQ, quarter)
        back_parts = (jnp.einsum('rqf,dqf->qrd', gate_q, wg_q) + jnp.einsum('rqf,dqf->qrd', up_q, wu_q)).astype(jnp.bfloat16)
        slot_back = lax.optimization_barrier(jnp.sum(back_parts.astype(jnp.float32), axis=0)).astype(jnp.bfloat16)
        return (slot_out, slot_back, gate_grad, up_grad, down_grad)
    slot_out, slot_back, w_gate_grad, w_up_grad, w_down_grad = lax.map(per_item, (table.reshape(EXPERTS, per_expert), w_gate, w_up, w_down))
    picked_out = slot_out.reshape(-1, D)[flat_index].astype(jnp.float32).reshape(TOKENS, TOP, D)
    picked_back = slot_back.reshape(-1, D)[flat_index].astype(jnp.float32).reshape(TOKENS, TOP, D)
    mixed = lax.optimization_barrier(jnp.sum(coef.reshape(TOKENS, TOP, 1) * picked_out, axis=1)).astype(jnp.bfloat16)
    normed_grad = lax.optimization_barrier(jnp.sum(picked_back, axis=1))
    gain_grad = lax.optimization_barrier(jnp.sum(normed_grad * tokens_wide * recip, axis=0))
    scaled = norm_gain[None, :] * normed_grad
    inner = lax.optimization_barrier(jnp.sum(scaled * tokens_wide, axis=1, keepdims=True))
    tokens_grad = (recip * scaled - tokens_wide * recip * recip * recip * inner / D).astype(jnp.bfloat16)
    return (mixed, tokens_grad, gain_grad, w_gate_grad, w_up_grad, w_down_grad)
```

```python
import functools

import jax
import jax.numpy as jnp
from jax import lax
from jax.experimental import pallas as pl
from jax.experimental.pallas import tpu as pltpu
from jax.sharding import PartitionSpec as P

RAMP = 8
CORES = 2
DEPTH = 4

gate_unit = 65536.0
norm_eps = 1e-06
META = 128
CHUNK = 1024


AXES = ("seq", "ep")


def contract_rows(left, right):
    return lax.dot_general(
        left, right, (((0,), (0,)), ((), ())), preferred_element_type=jnp.float32
    )


def contract_cols(left, right):
    return lax.dot_general(
        left, right, (((1,), (1,)), ((), ())), preferred_element_type=jnp.float32
    )


def matmul(left, right):
    return jnp.dot(left, right, preferred_element_type=jnp.float32)


class Torus:
    def __init__(self, seq_count, ep_count):
        self.nx = seq_count
        self.nc = CORES
        self.nz = DEPTH
        self.ny = ep_count // (CORES * DEPTH)
        self.count = seq_count * ep_count
        self.swap = self.nx == self.ny

    def place(self, i):
        core = i % self.nc
        y = i // self.nc % self.ny
        z = i // (self.nc * self.ny) % self.nz
        x = i // (self.nc * self.ny * self.nz)
        return [x, z, y, core]

    def index(self, x, z, y, core):
        return ((x * self.nz + z) * self.ny + y) * self.nc + core

    def axis(self, step, core):
        first = 0 if (self.swap and core == 1) else 2
        return (1, first, 2 - first, 3)[step]

    def size(self, step):
        return (self.nz, self.ny, self.nx, self.nc)[step]

    def pairs(self, step, shift):
        sizes = [self.nx, self.nz, self.ny, self.nc]
        found = []
        for i in range(self.count):
            spot = self.place(i)
            axis = self.axis(step, spot[3])
            spot[axis] = (spot[axis] + shift) % sizes[axis]
            found.append((i, self.index(*spot)))
        return found


def shift_rows(torus, rows, step, shift):
    return lax.ppermute(rows, AXES, torus.pairs(step, shift))


def gather(torus, rows, name):
    with jax.named_scope(f"{name}_z"):
        others = [shift_rows(torus, rows, 0, -shift) for shift in range(1, torus.nz)]
    line = jnp.concatenate([rows] + others, axis=0)
    with jax.named_scope(f"{name}_b"):
        second = [line] + [shift_rows(torus, line, 1, -shift) for shift in range(1, torus.size(1))]
    with jax.named_scope(f"{name}_c"):
        third = [second] + [
            [shift_rows(torus, piece, 2, -shift) for piece in second]
            for shift in range(1, torus.size(2))
        ]
    flat = [piece for row in third for piece in row]
    with jax.named_scope(f"{name}_d"):
        pair = [shift_rows(torus, piece, 3, 1) for piece in flat]
    return flat + pair


def wide_sum(parts):
    total = parts[0].astype(jnp.float32)
    for part in parts[1:]:
        total = total + part.astype(jnp.float32)
    return total


def scatter_sum(torus, parts, name):
    n3, n2 = torus.size(2), torus.size(1)
    each = parts[0][0].shape[0] // n2
    with jax.named_scope(f"{name}_d"):
        got = [None] * n3
        for s3 in reversed(range(n3)):
            got[s3] = shift_rows(torus, parts[1][s3], 3, 1)
    near = [
        [
            [parts[0][s3][s2 * each : (s2 + 1) * each], got[s3][s2 * each : (s2 + 1) * each]]
            for s2 in range(n2)
        ]
        for s3 in range(n3)
    ]
    with jax.named_scope(f"{name}_c"):
        for s2 in reversed(range(n2)):
            for s3 in range(1, n3):
                send = wide_sum(near[s3][s2]).astype(jnp.bfloat16)
                near[0][s2].append(shift_rows(torus, send, 2, s3))
    with jax.named_scope(f"{name}_b"):
        for s2 in range(1, n2):
            send = wide_sum(near[0][s2]).astype(jnp.bfloat16)
            near[0][0].append(shift_rows(torus, send, 1, s2))
    total = wide_sum(near[0][0])
    rows = each // torus.nz
    with jax.named_scope(f"{name}_z"):
        last = [total[:rows]]
        for shift in range(1, torus.nz):
            block = total[shift * rows : (shift + 1) * rows].astype(jnp.bfloat16)
            last.append(shift_rows(torus, block, 0, shift))
    return wide_sum(last)


def forward_kernel(*refs, pieces, steps, width, top):
    scal = refs[0]
    tok = refs[1 : 1 + pieces]
    meta = refs[1 + pieces : 1 + 2 * pieces]
    gain, wg, wu, wd = refs[1 + 2 * pieces : 5 + 2 * pieces]
    outs = refs[5 + 2 * pieces :]
    x_all, pre_gate, pre_up, hidden, side = outs[:5]
    parts = outs[5:-4]
    acc_g, acc_u, squares, scaled = outs[-4:]
    i = pl.program_id(0)
    each = tok[0].shape[0]

    @pl.when(i < steps)
    def _():
        g = gain[...]
        for p in range(pieces):
            spot = slice(p * each, (p + 1) * each)
            raw = tok[p][...]
            x_all[spot, :] = raw
            x = raw.astype(jnp.float32)
            scaled[spot, :] = (x * g).astype(jnp.bfloat16)
            sq = x * x
            part = sq[:, :META]
            for c in range(1, sq.shape[1] // META):
                part = part + sq[:, c * META : (c + 1) * META]
            squares[spot, :] = jnp.where(i == 0, part, squares[spot, :] + part)
        xs = scaled[...]
        got_g = matmul(xs, wg[...])
        got_u = matmul(xs, wu[...])

        @pl.when(i == 0)
        def _():
            acc_g[...] = got_g
            acc_u[...] = got_u

        @pl.when(i > 0)
        def _():
            acc_g[...] += got_g
            acc_u[...] += got_u

    @pl.when(i == steps - 1)
    def _():
        recip = lax.rsqrt(jnp.sum(squares[...], axis=1, keepdims=True) / width + norm_eps)
        expert = scal[0].astype(jnp.float32)
        ramp = scal[1].astype(jnp.float32)
        table = jnp.concatenate([m[...] for m in meta], axis=0).astype(jnp.float32)
        gates = table[:, top : 2 * top] * 256.0 + table[:, 2 * top : 3 * top]
        chosen = table[:, :top] == expert
        coef = jnp.sum(jnp.where(chosen, gates, 0.0), axis=1, keepdims=True)
        coef = coef / gate_unit * ramp / RAMP
        pg = recip * acc_g[...]
        pu = recip * acc_u[...]
        pre_gate[...] = pg
        pre_up[...] = pu
        hidden[...] = (coef * (pg * jax.nn.sigmoid(pg) * pu)).astype(jnp.bfloat16)
        lane = lax.broadcasted_iota(jnp.int32, side.shape, 1)
        side[...] = jnp.where(lane == 0, recip, jnp.where(lane == 1, coef, 0.0))

    @pl.when(i >= steps)
    def _():
        out = matmul(hidden[...], wd[...]).astype(jnp.bfloat16)
        size = parts[0].shape[0]
        for p, ref in enumerate(parts):
            ref[...] = out[p * size : (p + 1) * size]


def backward_kernel(*refs, pieces, steps):
    grad = refs[:pieces]
    wd, wg, wu, x_all, pre_gate, pre_up, side = refs[pieces : pieces + 7]
    outs = refs[pieces + 7 :]
    og_all, pre_grads, gain_part = outs[:3]
    parts = outs[3:-3]
    acc, gate_s, up_s = outs[-3:]
    i = pl.program_id(0)
    each = grad[0].shape[0]

    @pl.when(i < steps)
    def _():
        for p in range(pieces):
            og_all[p * each : (p + 1) * each, :] = grad[p][...]
        got = contract_cols(og_all[...], wd[...])

        @pl.when(i == 0)
        def _():
            acc[...] = got

        @pl.when(i > 0)
        def _():
            acc[...] += got

    @pl.when(i == steps - 1)
    def _():
        recip = side[:, 0:1]
        coef = side[:, 1:2]
        hidden_grad = coef * acc[...]
        pg = pre_gate[...]
        pu = pre_up[...]
        sigma = jax.nn.sigmoid(pg)
        gate_grad = hidden_grad * pu * sigma * (1.0 + pg * (1.0 - sigma))
        up_grad = hidden_grad * (pg * sigma)
        gate_s[...] = gate_grad.astype(jnp.bfloat16)
        up_s[...] = up_grad.astype(jnp.bfloat16)
        half = gate_grad.shape[1]
        pre_grads[:, :half] = (recip * gate_grad).astype(jnp.bfloat16)
        pre_grads[:, half:] = (recip * up_grad).astype(jnp.bfloat16)

    @pl.when(i >= steps)
    def _():
        back = contract_cols(gate_s[...], wg[...]) + contract_cols(up_s[...], wu[...])
        recip = side[:, 0:1]
        gain_part[...] = jnp.sum(back * (x_all[...].astype(jnp.float32) * recip), axis=0, keepdims=True)
        out = back.astype(jnp.bfloat16)
        size = parts[0].shape[0]
        for p, ref in enumerate(parts):
            ref[...] = out[p * size : (p + 1) * size]


def up_grads_kernel(x_all, gain, pre_grads, wg_grad, wu_grad):
    xs = (x_all[...].astype(jnp.float32) * gain[...]).astype(jnp.bfloat16)
    both = contract_rows(xs, pre_grads[...]).astype(jnp.bfloat16)
    half = wg_grad.shape[1]
    wg_grad[...] = both[:, :half]
    wu_grad[...] = both[:, half:]


def down_grad_kernel(hidden, og_all, wd_grad):
    wd_grad[...] = contract_rows(hidden[...], og_all[...]).astype(jnp.bfloat16)


def params():
    return pltpu.CompilerParams(dimension_semantics=("arbitrary",), vmem_limit_bytes=56 * 1024 * 1024)


def cost(flops, size):
    return pl.CostEstimate(flops=int(flops), bytes_accessed=int(size), transcendentals=0)


def forward(torus, tok, gain, wg, wu, wd, scal, top):
    width, hid = wg.shape
    steps = width // CHUNK
    pieces = len(tok)
    each = tok[0].shape[0]
    rows = pieces * each
    n3 = torus.size(2)
    size = rows // (CORES * n3)
    first = lambda i: jnp.minimum(i, steps - 1)
    later = lambda i: jnp.maximum(i - steps, 0)
    fixed = lambda i: (0, 0)
    outs = pl.pallas_call(
        functools.partial(forward_kernel, pieces=pieces, steps=steps, width=width, top=top),
        grid=(2 * steps,),
        in_specs=[pl.BlockSpec(memory_space=pltpu.SMEM)]
        + [pl.BlockSpec((each, CHUNK), lambda i: (0, first(i)))] * pieces
        + [pl.BlockSpec((each, META), lambda i: (0, width // META))] * pieces
        + [
            pl.BlockSpec((1, CHUNK), lambda i: (0, first(i))),
            pl.BlockSpec((CHUNK, hid), lambda i: (first(i), 0)),
            pl.BlockSpec((CHUNK, hid), lambda i: (first(i), 0)),
            pl.BlockSpec((hid, CHUNK), lambda i: (0, later(i))),
        ],
        out_specs=[
            pl.BlockSpec((rows, CHUNK), lambda i: (0, first(i))),
            pl.BlockSpec((rows, hid), fixed),
            pl.BlockSpec((rows, hid), fixed),
            pl.BlockSpec((rows, hid), fixed),
            pl.BlockSpec((rows, META), fixed),
        ]
        + [pl.BlockSpec((size, CHUNK), lambda i: (0, later(i)))] * (CORES * n3),
        out_shape=[
            jax.ShapeDtypeStruct((rows, width), jnp.bfloat16),
            jax.ShapeDtypeStruct((rows, hid), jnp.float32),
            jax.ShapeDtypeStruct((rows, hid), jnp.float32),
            jax.ShapeDtypeStruct((rows, hid), jnp.bfloat16),
            jax.ShapeDtypeStruct((rows, META), jnp.float32),
        ]
        + [jax.ShapeDtypeStruct((size, width), jnp.bfloat16)] * (CORES * n3),
        scratch_shapes=[
            pltpu.VMEM((rows, hid), jnp.float32),
            pltpu.VMEM((rows, hid), jnp.float32),
            pltpu.VMEM((rows, META), jnp.float32),
            pltpu.VMEM((rows, CHUNK), jnp.bfloat16),
        ],
        compiler_params=params(),
        cost_estimate=cost(6 * rows * width * hid, 6 * width * hid + 6 * rows * width),
        name="forward",
    )(scal, *tok, *tok, gain, wg, wu, wd)
    x_all, pre_gate, pre_up, hidden, side = outs[:5]
    parts = [outs[5 + c * n3 : 5 + (c + 1) * n3] for c in range(CORES)]
    return x_all, pre_gate, pre_up, hidden, side, parts


def backward(torus, grad, wd, wg, wu, x_all, pre_gate, pre_up, side):
    width, hid = wg.shape
    steps = width // CHUNK
    pieces = len(grad)
    each = grad[0].shape[0]
    rows = pieces * each
    n3 = torus.size(2)
    size = rows // (CORES * n3)
    first = lambda i: jnp.minimum(i, steps - 1)
    later = lambda i: jnp.maximum(i - steps, 0)
    fixed = lambda i: (0, 0)
    outs = pl.pallas_call(
        functools.partial(backward_kernel, pieces=pieces, steps=steps),
        grid=(2 * steps,),
        in_specs=[pl.BlockSpec((each, CHUNK), lambda i: (0, first(i)))] * pieces
        + [
            pl.BlockSpec((hid, CHUNK), lambda i: (0, first(i))),
            pl.BlockSpec((CHUNK, hid), lambda i: (later(i), 0)),
            pl.BlockSpec((CHUNK, hid), lambda i: (later(i), 0)),
            pl.BlockSpec((rows, CHUNK), lambda i: (0, later(i))),
            pl.BlockSpec((rows, hid), fixed),
            pl.BlockSpec((rows, hid), fixed),
            pl.BlockSpec((rows, META), fixed),
        ],
        out_specs=[
            pl.BlockSpec((rows, CHUNK), lambda i: (0, first(i))),
            pl.BlockSpec((rows, 2 * hid), fixed),
            pl.BlockSpec((1, CHUNK), lambda i: (0, later(i))),
        ]
        + [pl.BlockSpec((size, CHUNK), lambda i: (0, later(i)))] * (CORES * n3),
        out_shape=[
            jax.ShapeDtypeStruct((rows, width), jnp.bfloat16),
            jax.ShapeDtypeStruct((rows, 2 * hid), jnp.bfloat16),
            jax.ShapeDtypeStruct((1, width), jnp.float32),
        ]
        + [jax.ShapeDtypeStruct((size, width), jnp.bfloat16)] * (CORES * n3),
        scratch_shapes=[
            pltpu.VMEM((rows, hid), jnp.float32),
            pltpu.VMEM((rows, hid), jnp.bfloat16),
            pltpu.VMEM((rows, hid), jnp.bfloat16),
        ],
        compiler_params=params(),
        cost_estimate=cost(6 * rows * width * hid, 6 * width * hid + 6 * rows * width),
        name="backward",
    )(*grad, wd, wg, wu, x_all, pre_gate, pre_up, side)
    parts = [outs[3 + c * n3 : 3 + (c + 1) * n3] for c in range(CORES)]
    return outs[0], outs[1], outs[2], parts


def up_grads(x_all, gain, pre_grads):
    rows, width = x_all.shape
    hid = pre_grads.shape[1] // 2
    return pl.pallas_call(
        up_grads_kernel,
        grid=(width // CHUNK,),
        in_specs=[
            pl.BlockSpec((rows, CHUNK), lambda i: (0, i)),
            pl.BlockSpec((1, CHUNK), lambda i: (0, i)),
            pl.BlockSpec((rows, 2 * hid), lambda i: (0, 0)),
        ],
        out_specs=[pl.BlockSpec((CHUNK, hid), lambda i: (i, 0))] * 2,
        out_shape=[jax.ShapeDtypeStruct((width, hid), jnp.bfloat16)] * 2,
        compiler_params=params(),
        cost_estimate=cost(4 * rows * width * hid, 4 * width * hid + 2 * rows * width),
        name="up_grads",
    )(x_all, gain, pre_grads)


def down_grad(hidden, og_all):
    rows, width = og_all.shape
    hid = hidden.shape[1]
    return pl.pallas_call(
        down_grad_kernel,
        grid=(width // CHUNK,),
        in_specs=[
            pl.BlockSpec((rows, hid), lambda i: (0, 0)),
            pl.BlockSpec((rows, CHUNK), lambda i: (0, i)),
        ],
        out_specs=pl.BlockSpec((hid, CHUNK), lambda i: (0, i)),
        out_shape=jax.ShapeDtypeStruct((hid, width), jnp.bfloat16),
        compiler_params=params(),
        cost_estimate=cost(2 * rows * width * hid, 2 * width * hid + 2 * rows * width),
        name="down_grad",
    )(hidden, og_all)


def on_device(tokens, out_grad, routes, gate_fixed, ramp_step, norm_gain, w_gate, w_up, w_down):
    seq_count = lax.axis_size("seq")
    ep_count = lax.axis_size("ep")
    torus = Torus(seq_count, ep_count)
    width = tokens.shape[1]
    top = routes.shape[1]
    high = gate_fixed // 256
    meta = jnp.concatenate([routes, high, gate_fixed - 256 * high], axis=1)
    meta = jnp.pad(meta, ((0, 0), (0, META - 3 * top))).astype(jnp.bfloat16)
    tok = gather(torus, jnp.concatenate([tokens, meta], axis=1), "tok")
    grad = gather(torus, out_grad, "grad")
    expert = lax.axis_index("ep")
    scal = jnp.stack([expert, ramp_step[expert]])
    gain = norm_gain[None, :]
    wg, wu, wd = w_gate[0], w_up[0], w_down[0]
    with jax.named_scope("k_forward"):
        x_all, pre_gate, pre_up, hidden, side, parts = forward(torus, tok, gain, wg, wu, wd, scal, top)
    mixed = scatter_sum(torus, parts, "out").astype(jnp.bfloat16)
    with jax.named_scope("k_backward"):
        og_all, pre_grads, gain_part, parts = backward(
            torus, grad, wd, wg, wu, x_all, pre_gate, pre_up, side
        )
    with jax.named_scope("gain_sum"):
        gain_all = lax.all_to_all(
            gain_part.reshape(seq_count * ep_count, -1), AXES, split_axis=0, concat_axis=0, tiled=True
        )
        gain_grad = jnp.sum(gain_all, axis=0)
    normed_grad = scatter_sum(torus, parts, "back")
    with jax.named_scope("k_down_grad"):
        w_down_grad = down_grad(hidden, og_all)[None]
    with jax.named_scope("k_up_grads"):
        w_gate_grad, w_up_grad = up_grads(x_all, gain, pre_grads)
    own = tokens.astype(jnp.float32)
    own_recip = lax.rsqrt(jnp.mean(own * own, axis=1, keepdims=True) + norm_eps)
    scaled = gain * normed_grad
    inner = jnp.sum(scaled * own, axis=1, keepdims=True)
    tokens_grad = (
        own_recip * scaled - own * own_recip * own_recip * own_recip * inner / width
    ).astype(jnp.bfloat16)
    return (mixed, tokens_grad, gain_grad, w_gate_grad[None], w_up_grad[None], w_down_grad)


def solution(mesh):
    return jax.shard_map(
        on_device,
        mesh=mesh,
        in_specs=(
            P(("seq", "ep"), None),
            P(("seq", "ep"), None),
            P(("seq", "ep"), None),
            P(("seq", "ep"), None),
            P(),
            P(),
            P("ep", None, "seq"),
            P("ep", None, "seq"),
            P("ep", "seq", None),
        ),
        out_specs=(
            P(("seq", "ep"), None),
            P(("seq", "ep"), None),
            P(("seq", "ep")),
            P("ep", None, "seq"),
            P("ep", None, "seq"),
            P("ep", "seq", None),
        ),
        check_vma=False,
    )
```

```python
import functools

import jax
import jax.numpy as jnp
from jax import lax
from jax.experimental import pallas as pl
from jax.experimental.pallas import tpu as pltpu
from jax.sharding import PartitionSpec as P


RAMP = 8
CORES = 2
DEPTH = 4

gate_unit = 65536.0
norm_eps = 1e-06
META = 128
CHUNK = 1024
WIDE = 1792
WHOLE_ROWS = 256
VMEM_MIB = 14


AXES = ("seq", "ep")


def contract_rows(left, right):
    return lax.dot_general(
        left, right, (((0,), (0,)), ((), ())), preferred_element_type=jnp.float32
    )


def contract_cols(left, right):
    return lax.dot_general(
        left, right, (((1,), (1,)), ((), ())), preferred_element_type=jnp.float32
    )


def matmul(left, right):
    return jnp.dot(left, right, preferred_element_type=jnp.float32)


class Torus:
    def __init__(self, seq_count, ep_count):
        self.nx = seq_count
        self.nc = CORES
        self.nz = DEPTH
        self.ny = ep_count // (CORES * DEPTH)
        self.count = seq_count * ep_count
        self.swap = self.nx == self.ny

    def place(self, i):
        core = i % self.nc
        y = i // self.nc % self.ny
        z = i // (self.nc * self.ny) % self.nz
        x = i // (self.nc * self.ny * self.nz)
        return [x, z, y, core]

    def index(self, x, z, y, core):
        return ((x * self.nz + z) * self.ny + y) * self.nc + core

    def axis(self, step, core):
        first = 0 if (self.swap and core == 1) else 2
        return (1, first, 2 - first, 3)[step]

    def size(self, step):
        return (self.nz, self.ny, self.nx, self.nc)[step]

    def pairs(self, step, shift):
        sizes = [self.nx, self.nz, self.ny, self.nc]
        found = []
        for i in range(self.count):
            spot = self.place(i)
            axis = self.axis(step, spot[3])
            spot[axis] ^= shift
            found.append((i, self.index(*spot)))
        return found

    def check(self):
        assert all(n & (n - 1) == 0 for n in (self.nx, self.ny, self.nz, self.nc))


def shift_rows(torus, rows, step, shift):
    return lax.ppermute(rows, AXES, torus.pairs(step, shift))


def planes(torus, rows):
    second = [rows] + [shift_rows(torus, rows, 1, s) for s in range(1, torus.size(1))]
    third = [second] + [
        [shift_rows(torus, piece, 2, s) for piece in second]
        for s in range(1, torus.size(2))
    ]
    return [piece for row in third for piece in row]


def gather(torus, rows):
    near = jnp.concatenate(planes(torus, rows), axis=0)
    near_pair = shift_rows(torus, near, 3, 1)
    others = [shift_rows(torus, rows, 0, s) for s in range(1, torus.nz)]
    far = planes(torus, jnp.concatenate(others, axis=0))
    far_pair = [shift_rows(torus, piece, 3, 1) for piece in far]
    return far + far_pair + [near, near_pair]


def load_rows(refs, cols):
    far, near = refs[:-2], refs[-2:]
    half = len(far) // CORES
    own = near[0].shape[0] // half
    found = []
    for core in range(CORES):
        block = near[core][:, cols].astype(jnp.float32)
        for k in range(half):
            wide = far[core * half + k][:, cols].astype(jnp.float32)
            found.append(jnp.concatenate([wide, block[k * own : (k + 1) * own]], axis=0))
    return found


def wide_sum(parts):
    total = parts[0].astype(jnp.float32)
    for part in parts[1:]:
        total = total + part.astype(jnp.float32)
    return total


def scatter_sum(torus, parts, after=None):
    n3, n2 = torus.size(2), torus.size(1)
    each = parts[0][0].shape[0] // n2
    got = [None] * n3
    for s3 in reversed(range(n3)):
        got[s3] = shift_rows(torus, parts[1][s3], 3, 1)
    near = [
        [
            [parts[0][s3][s2 * each : (s2 + 1) * each], got[s3][s2 * each : (s2 + 1) * each]]
            for s2 in range(n2)
        ]
        for s3 in range(n3)
    ]
    for s2 in reversed(range(n2)):
        for s3 in range(1, n3):
            send = wide_sum(near[s3][s2]).astype(jnp.bfloat16)
            near[0][s2].append(shift_rows(torus, send, 2, s3))
    for s2 in range(1, n2):
        send = wide_sum(near[0][s2]).astype(jnp.bfloat16)
        near[0][0].append(shift_rows(torus, send, 1, s2))
    if after is not None:
        near[0][0][-1], after = lax.optimization_barrier((near[0][0][-1], after))
    total = wide_sum(near[0][0])
    rows = each // torus.nz
    last = [total[each - rows :]]
    for shift in reversed(range(1, torus.nz)):
        block = total[(shift - 1) * rows : shift * rows].astype(jnp.bfloat16)
        last.append(shift_rows(torus, block, 0, shift))
    return wide_sum(last) if after is None else (wide_sum(last), after)


def gain_rows(span):
    return (span + 2 * META - 2) // META


def gain_tiles(torus, device, gain_ref, span, rows):
    count = gain_rows(span)
    core = device % CORES
    tiles = []
    for other in range(CORES):
        odd = (core + other) % CORES
        for s3 in range(torus.size(2)):
            for s2 in range(torus.size(1)):
                for sz in [*range(1, torus.nz), 0]:
                    even_mask = torus.index(s3, sz, s2, other)
                    odd_mask = torus.index(s2, sz, s3, other) if torus.swap else even_mask
                    target = device ^ jnp.where(odd == 1, odd_mask, even_mask)
                    value = gain_ref[pl.ds(target * span // META, count), :]
                    high = value.astype(jnp.bfloat16).astype(jnp.float32)
                    rest = jnp.zeros((rows - 2 * count, META), jnp.float32)
                    tiles.append(jnp.concatenate([high, value - high, rest], axis=0))
    return tiles


def gates_of(table, place, ramp_step, top):
    place = place.astype(jnp.int32)
    expert = place.astype(jnp.float32)
    ramp = ramp_step[place].astype(jnp.float32)
    gates = table[:, top : 2 * top] * 256.0 + table[:, 2 * top : 3 * top]
    coef = jnp.sum(jnp.where(table[:, :top] == expert, gates, 0.0), axis=1, keepdims=True)
    return coef / gate_unit * ramp / RAMP


def fold_lanes(rows):
    part = rows[:, :META]
    for c in range(1, rows.shape[1] // META):
        part = part + rows[:, c * META : (c + 1) * META]
    return part


def pack_kernel(tokens, routes, gates, out, meta):
    width = tokens.shape[1]
    top = routes.shape[1]
    out[:, :width] = tokens[...]
    fixed = gates[...]
    high = fixed // 256
    meta[...] = jnp.zeros_like(meta)
    meta[:, :top] = routes[...].astype(jnp.float32)
    meta[:, top : 2 * top] = high.astype(jnp.float32)
    meta[:, 2 * top : 3 * top] = (fixed - 256 * high).astype(jnp.float32)
    out[:, width:] = meta[...].astype(jnp.bfloat16)


def pack(tokens, routes, gates):
    rows, width = tokens.shape
    vmem = pl.BlockSpec(memory_space=pltpu.VMEM)
    return pl.pallas_call(
        pack_kernel,
        in_specs=[vmem] * 3,
        out_specs=vmem,
        out_shape=jax.ShapeDtypeStruct((rows, width + META), jnp.bfloat16),
        scratch_shapes=[pltpu.VMEM((rows, META), jnp.float32)],
        compiler_params=pltpu.CompilerParams(vmem_limit_bytes=4 * 2**20),
        name="pack",
    )(*off_chip(tokens, routes, gates))


def send_parts(rows, parts, cols, sems, first):
    size = parts[0].shape[0]
    copies = [
        pltpu.make_async_copy(
            rows.at[p * size : (p + 1) * size, cols], ref.at[:, cols], sems.at[first + p]
        )
        for p, ref in enumerate(parts)
    ]
    for copy in copies:
        copy.start()
    return copies


def forward_whole(*refs, pieces, width, top):
    spot, ramp_step = refs[:2]
    tok = refs[2 : 2 + pieces]
    gain, wg, wu, wd = refs[2 + pieces : 6 + pieces]
    outs = refs[6 + pieces :]
    scaled, pre_gate, pre_up, hidden, side = outs[:5]
    parts = outs[5:-4]
    acc_g, acc_u, sums, sems = outs[-4:]
    pending = []
    squares = []
    for k in range(width // WIDE):
        cols = slice(k * WIDE, (k + 1) * WIDE)
        g = gain[:, cols]
        for p, x in enumerate(load_rows(tok, cols)):
            each = x.shape[0]
            scaled[p * each : (p + 1) * each, cols] = (x * g).astype(jnp.bfloat16)
            part = fold_lanes(x * x)
            if k == 0:
                squares.append(part)
            else:
                squares[p] = squares[p] + part
        xs = scaled[:, cols]
        if k == 0:
            acc_g[...] = matmul(xs, wg[cols, :])
            acc_u[...] = matmul(xs, wu[cols, :])
        else:
            acc_g[...] += matmul(xs, wg[cols, :])
            acc_u[...] += matmul(xs, wu[cols, :])
    total = jnp.sum(jnp.concatenate(squares, axis=0), axis=1, keepdims=True)
    recip = lax.rsqrt(total / width + norm_eps)
    table = jnp.concatenate(load_rows(tok, slice(width, width + META)), axis=0)
    coef = gates_of(table, spot[0], ramp_step, top)
    pg = recip * acc_g[...]
    pu = recip * acc_u[...]
    pre_gate[...] = pg
    pre_up[...] = pu
    hidden[...] = (coef * (pg * jax.nn.sigmoid(pg) * pu)).astype(jnp.bfloat16)
    lane = lax.broadcasted_iota(jnp.int32, side.shape, 1)
    side[...] = jnp.where(lane == 0, recip, jnp.where(lane == 1, coef, 0.0))
    for k in range(width // WIDE):
        cols = slice(k * WIDE, (k + 1) * WIDE)
        sums[:, cols] = matmul(hidden[...], wd[:, cols]).astype(jnp.bfloat16)
        pending += send_parts(sums, parts, cols, sems, k * len(parts))
    for copy in pending:
        copy.wait()


def backward_whole(*refs, pieces, width, torus):
    spot = refs[0]
    grad = refs[1 : 1 + pieces]
    tok = refs[1 + pieces : 1 + 2 * pieces]
    wd, wg, wu, pre_gate, pre_up, side = refs[1 + 2 * pieces : 7 + 2 * pieces]
    outs = refs[7 + 2 * pieces :]
    og_all, pre_grads = outs[:2]
    parts = outs[2:-6]
    acc, gate_s, up_s, sums, gain_ref, sems = outs[-6:]
    pending = []
    steps = width // WIDE
    for k in range(steps):
        cols = slice(k * WIDE, (k + 1) * WIDE)
        for p, rows in enumerate(load_rows(grad, cols)):
            each = rows.shape[0]
            og_all[p * each : (p + 1) * each, cols] = rows.astype(jnp.bfloat16)
        got = contract_cols(og_all[:, cols], wd[:, cols])
        if k == 0:
            acc[...] = got
        else:
            acc[...] += got
    recip = side[:, 0:1]
    coef = side[:, 1:2]
    pre_grads_of(acc, pre_gate, pre_up, recip, coef, gate_s, up_s, pre_grads)
    gain_ref[...] = jnp.zeros_like(gain_ref)
    for k in range(steps):
        cols = slice(k * WIDE, (k + 1) * WIDE)
        back = contract_cols(gate_s[...], wg[cols, :]) + contract_cols(up_s[...], wu[cols, :])
        sums[:, cols] = back.astype(jnp.bfloat16)
        total = None
        for p, x in enumerate(load_rows(tok, cols)):
            each = x.shape[0]
            rows = slice(p * each, (p + 1) * each)
            part = back[rows] * (x * recip[rows])
            total = part if p == 0 else total + part
        keep_gain(gain_ref, total, k * WIDE // META)
        if k == steps - 1:
            sums[:, width:] = gain_block(torus, spot, gain_ref, width, recip.shape[0])
            cols = slice(k * WIDE, width + META)
        pending += send_parts(sums, parts, cols, sems, steps + k * len(parts))
    for copy in pending:
        copy.wait()


def keep_gain(gain_ref, total, first):
    row = jnp.sum(total, axis=0, keepdims=True)
    for c in range(row.shape[1] // META):
        gain_ref[first + c : first + c + 1, :] = row[:, c * META : (c + 1) * META]


def gain_block(torus, spot, gain_ref, width, rows):
    device = spot[1].astype(jnp.int32)
    tiles = gain_tiles(torus, device, gain_ref, width // torus.count, rows // torus.count)
    return jnp.concatenate(tiles, axis=0).astype(jnp.bfloat16)


def prefetch_kernel(_, *refs):
    count = len(refs) // 2
    sems = refs[-1]
    copies = [
        pltpu.make_async_copy(refs[k], refs[count + k], sems.at[k]) for k in range(count)
    ]
    for copy in copies:
        copy.start()
    for copy in copies:
        copy.wait()


def off_chip(*arrays):
    return [pltpu.with_memory_space_constraint(a, pltpu.HBM) for a in arrays]


def on_chip(*arrays):
    return [pltpu.with_memory_space_constraint(a, pltpu.VMEM) for a in arrays]


def prefetch(spot, weights):
    return pl.pallas_call(
        prefetch_kernel,
        in_specs=[pl.BlockSpec(memory_space=pltpu.SMEM)]
        + [pl.BlockSpec(memory_space=pltpu.HBM)] * len(weights),
        out_specs=[pl.BlockSpec(memory_space=pltpu.VMEM)] * len(weights),
        out_shape=[pltpu.VMEM(w.shape, w.dtype) for w in weights],
        scratch_shapes=[pltpu.SemaphoreType.DMA((len(weights),))],
        compiler_params=pltpu.CompilerParams(vmem_limit_bytes=2**20),
        name="prefetch",
    )(spot, *off_chip(*weights))


def pre_grads_of(acc, pre_gate, pre_up, recip, coef, gate_s, up_s, pre_grads):
    hidden_grad = coef * acc[...]
    pg = pre_gate[...]
    pu = pre_up[...]
    sigma = jax.nn.sigmoid(pg)
    gate_grad = hidden_grad * pu * sigma * (1.0 + pg * (1.0 - sigma))
    up_grad = hidden_grad * (pg * sigma)
    gate_s[...] = gate_grad.astype(jnp.bfloat16)
    up_s[...] = up_grad.astype(jnp.bfloat16)
    half = gate_grad.shape[1]
    pre_grads[:, :half] = (recip * gate_grad).astype(jnp.bfloat16)
    pre_grads[:, half:] = (recip * up_grad).astype(jnp.bfloat16)


def forward_kernel(*refs, pieces, steps, width, top):
    spot, ramp_step = refs[:2]
    tok = refs[2 : 2 + pieces]
    meta = refs[2 + pieces : 2 + 2 * pieces]
    gain, wg, wu, wd = refs[2 + 2 * pieces : 6 + 2 * pieces]
    outs = refs[6 + 2 * pieces :]
    scaled, pre_gate, pre_up, hidden, side = outs[:5]
    parts = outs[5:-3]
    acc_g, acc_u, squares = outs[-3:]
    i = pl.program_id(0)

    @pl.when(i < steps)
    def _():
        g = gain[...]
        for p, x in enumerate(load_rows(tok, slice(None))):
            each = x.shape[0]
            part_rows = slice(p * each, (p + 1) * each)
            scaled[part_rows, :] = (x * g).astype(jnp.bfloat16)
            part = fold_lanes(x * x)
            squares[part_rows, :] = jnp.where(i == 0, part, squares[part_rows, :] + part)
        xs = scaled[...]
        got_g = matmul(xs, wg[...])
        got_u = matmul(xs, wu[...])

        @pl.when(i == 0)
        def _():
            acc_g[...] = got_g
            acc_u[...] = got_u

        @pl.when(i > 0)
        def _():
            acc_g[...] += got_g
            acc_u[...] += got_u

    @pl.when(i == steps - 1)
    def _():
        recip = lax.rsqrt(jnp.sum(squares[...], axis=1, keepdims=True) / width + norm_eps)
        table = jnp.concatenate(load_rows(meta, slice(None)), axis=0)
        coef = gates_of(table, spot[0], ramp_step, top)
        pg = recip * acc_g[...]
        pu = recip * acc_u[...]
        pre_gate[...] = pg
        pre_up[...] = pu
        hidden[...] = (coef * (pg * jax.nn.sigmoid(pg) * pu)).astype(jnp.bfloat16)
        lane = lax.broadcasted_iota(jnp.int32, side.shape, 1)
        side[...] = jnp.where(lane == 0, recip, jnp.where(lane == 1, coef, 0.0))

    @pl.when(i >= steps)
    def _():
        out = matmul(hidden[...], wd[...]).astype(jnp.bfloat16)
        size = parts[0].shape[0]
        for p, ref in enumerate(parts):
            ref[...] = out[p * size : (p + 1) * size]


def backward_kernel(*refs, pieces, steps, width, torus):
    spot = refs[0]
    grad = refs[1 : 1 + pieces]
    tok = refs[1 + pieces : 1 + 2 * pieces]
    wd, wg, wu, pre_gate, pre_up, side = refs[1 + 2 * pieces : 7 + 2 * pieces]
    outs = refs[7 + 2 * pieces :]
    og_all, pre_grads = outs[:2]
    parts = outs[2:-4]
    acc, gate_s, up_s, gain_ref = outs[-4:]
    i = pl.program_id(0)
    size = parts[0].shape[0]

    @pl.when(i < steps)
    def _():
        for p, rows in enumerate(load_rows(grad, slice(None))):
            each = rows.shape[0]
            og_all[p * each : (p + 1) * each, :] = rows.astype(jnp.bfloat16)
        got = contract_cols(og_all[...], wd[...])

        @pl.when(i == 0)
        def _():
            acc[...] = got
            gain_ref[...] = jnp.zeros_like(gain_ref)

        @pl.when(i > 0)
        def _():
            acc[...] += got

    @pl.when(i == steps - 1)
    def _():
        recip = side[:, 0:1]
        coef = side[:, 1:2]
        pre_grads_of(acc, pre_gate, pre_up, recip, coef, gate_s, up_s, pre_grads)

    for k in range(steps):

        @pl.when(i == steps + k)
        def _(k=k):
            back = contract_cols(gate_s[...], wg[...]) + contract_cols(up_s[...], wu[...])
            recip = side[:, 0:1]
            total = None
            for p, x in enumerate(load_rows(tok, slice(None))):
                each = x.shape[0]
                rows = slice(p * each, (p + 1) * each)
                part = back[rows] * (x * recip[rows])
                total = part if p == 0 else total + part
            keep_gain(gain_ref, total, k * CHUNK // META)
            out = back.astype(jnp.bfloat16)
            for p, ref in enumerate(parts):
                ref[...] = out[p * size : (p + 1) * size]

    @pl.when(i == 2 * steps)
    def _():
        out = gain_block(torus, spot, gain_ref, width, side.shape[0])
        for p, ref in enumerate(parts):
            ref[:, :META] = out[p * size : (p + 1) * size]


def up_grads_kernel(scaled, pre_grads, wg_grad, wu_grad):
    both = contract_rows(scaled[...], pre_grads[...]).astype(jnp.bfloat16)
    half = wg_grad.shape[1]
    wg_grad[...] = both[:, :half]
    wu_grad[...] = both[:, half:]


def down_grad_kernel(hidden, og_all, wd_grad):
    wd_grad[...] = contract_rows(hidden[...], og_all[...]).astype(jnp.bfloat16)


def params(mib=56):
    return pltpu.CompilerParams(dimension_semantics=("arbitrary",), vmem_limit_bytes=mib * 2**20)


def placed(shapes, low, high):
    return [
        (pltpu.VMEM if low <= k < high else pltpu.HBM)(s.shape, s.dtype)
        for k, s in enumerate(shapes)
    ]


def shapes_of(rows, width, hid, size, parts):
    scratch = [
        jax.ShapeDtypeStruct((rows, width), jnp.bfloat16),
        jax.ShapeDtypeStruct((rows, hid), jnp.float32),
        jax.ShapeDtypeStruct((rows, hid), jnp.float32),
        jax.ShapeDtypeStruct((rows, hid), jnp.bfloat16),
        jax.ShapeDtypeStruct((rows, META), jnp.float32),
    ]
    return scratch + [jax.ShapeDtypeStruct((size, width), jnp.bfloat16)] * parts


def cost(flops, size):
    return pl.CostEstimate(flops=int(flops), bytes_accessed=int(size), transcendentals=0)


def forward(torus, tok, gain, wg, wu, wd, spot, ramp_step, top):
    width, hid = wg.shape
    steps = width // CHUNK
    pieces = len(tok)
    heights = [t.shape[0] for t in tok]
    rows = sum(heights)
    n3 = torus.size(2)
    size = rows // (CORES * n3)
    first = lambda i: jnp.minimum(i, steps - 1)
    later = lambda i: jnp.maximum(i - steps, 0)
    fixed = lambda i: (0, 0)
    if rows <= WHOLE_ROWS:
        vmem = pl.BlockSpec(memory_space=pltpu.VMEM)
        hbm = pl.BlockSpec(memory_space=pltpu.HBM)
        outs = pl.pallas_call(
            functools.partial(forward_whole, pieces=pieces, width=width, top=top),
            in_specs=[pl.BlockSpec(memory_space=pltpu.SMEM)] * 2 + [vmem] * (pieces + 4),
            out_specs=[vmem] * 5 + [hbm] * (CORES * n3),
            out_shape=placed(shapes_of(rows, width, hid, size, CORES * n3), 0, 5),
            scratch_shapes=[
                pltpu.VMEM((rows, hid), jnp.float32),
                pltpu.VMEM((rows, hid), jnp.float32),
                pltpu.VMEM((rows, width), jnp.bfloat16),
                pltpu.SemaphoreType.DMA((width // WIDE * (1 + CORES * n3),)),
            ],
            compiler_params=pltpu.CompilerParams(vmem_limit_bytes=VMEM_MIB * 2**20),
            cost_estimate=cost(6 * rows * width * hid, 6 * width * hid + 6 * rows * width),
            name="forward",
        )(spot, ramp_step, *tok, gain, *on_chip(wg, wu, wd))
        return (*outs[:5], [outs[5 + c * n3 : 5 + (c + 1) * n3] for c in range(CORES)])
    outs = pl.pallas_call(
        functools.partial(forward_kernel, pieces=pieces, steps=steps, width=width, top=top),
        grid=(2 * steps,),
        in_specs=[pl.BlockSpec(memory_space=pltpu.SMEM)] * 2
        + [pl.BlockSpec((h, CHUNK), lambda i: (0, first(i))) for h in heights]
        + [pl.BlockSpec((h, META), lambda i: (0, width // META)) for h in heights]
        + [
            pl.BlockSpec((1, CHUNK), lambda i: (0, first(i))),
            pl.BlockSpec((CHUNK, hid), lambda i: (first(i), 0)),
            pl.BlockSpec((CHUNK, hid), lambda i: (first(i), 0)),
            pl.BlockSpec((hid, CHUNK), lambda i: (0, later(i))),
        ],
        out_specs=[
            pl.BlockSpec((rows, CHUNK), lambda i: (0, first(i))),
            pl.BlockSpec((rows, hid), fixed),
            pl.BlockSpec((rows, hid), fixed),
            pl.BlockSpec((rows, hid), fixed),
            pl.BlockSpec((rows, META), fixed),
        ]
        + [pl.BlockSpec((size, CHUNK), lambda i: (0, later(i)))] * (CORES * n3),
        out_shape=shapes_of(rows, width, hid, size, CORES * n3),
        scratch_shapes=[
            pltpu.VMEM((rows, hid), jnp.float32),
            pltpu.VMEM((rows, hid), jnp.float32),
            pltpu.VMEM((rows, META), jnp.float32),
        ],
        compiler_params=params(),
        cost_estimate=cost(6 * rows * width * hid, 6 * width * hid + 6 * rows * width),
        name="forward",
    )(spot, ramp_step, *tok, *tok, gain, wg, wu, wd)
    scaled, pre_gate, pre_up, hidden, side = outs[:5]
    parts = [outs[5 + c * n3 : 5 + (c + 1) * n3] for c in range(CORES)]
    return scaled, pre_gate, pre_up, hidden, side, parts


def backward(torus, spot, grad, tok, wd, wg, wu, pre_gate, pre_up, side):
    width, hid = wg.shape
    steps = width // CHUNK
    pieces = len(grad)
    heights = [g.shape[0] for g in grad]
    rows = sum(heights)
    n3 = torus.size(2)
    size = rows // (CORES * n3)
    first = lambda i: jnp.minimum(i, steps - 1)
    later = lambda i: jnp.maximum(i - steps, 0)
    held = lambda i: jnp.clip(i - steps, 0, steps - 1)
    fixed = lambda i: (0, 0)
    shapes = [
        jax.ShapeDtypeStruct((rows, width), jnp.bfloat16),
        jax.ShapeDtypeStruct((rows, 2 * hid), jnp.bfloat16),
    ] + [jax.ShapeDtypeStruct((size, width + META), jnp.bfloat16)] * (CORES * n3)
    if rows <= WHOLE_ROWS:
        vmem = pl.BlockSpec(memory_space=pltpu.VMEM)
        hbm = pl.BlockSpec(memory_space=pltpu.HBM)
        outs = pl.pallas_call(
            functools.partial(backward_whole, pieces=pieces, width=width, torus=torus),
            in_specs=[pl.BlockSpec(memory_space=pltpu.SMEM)] + [vmem] * (2 * pieces + 6),
            out_specs=[vmem, vmem] + [hbm] * (CORES * n3),
            out_shape=placed(shapes, 0, 2),
            scratch_shapes=[
                pltpu.VMEM((rows, hid), jnp.float32),
                pltpu.VMEM((rows, hid), jnp.bfloat16),
                pltpu.VMEM((rows, hid), jnp.bfloat16),
                pltpu.VMEM((rows, width + META), jnp.bfloat16),
                pltpu.VMEM((width // META + 8, META), jnp.float32),
                pltpu.SemaphoreType.DMA((width // WIDE * (1 + CORES * n3),)),
            ],
            compiler_params=pltpu.CompilerParams(vmem_limit_bytes=VMEM_MIB * 2**20),
            cost_estimate=cost(6 * rows * width * hid, 6 * width * hid + 6 * rows * width),
            name="backward",
        )(spot, *grad, *tok, *on_chip(wd, wg, wu, pre_gate, pre_up, side))
        return (*outs[:2], [outs[2 + c * n3 : 2 + (c + 1) * n3] for c in range(CORES)])
    outs = pl.pallas_call(
        functools.partial(backward_kernel, pieces=pieces, steps=steps, width=width, torus=torus),
        grid=(2 * steps + 1,),
        in_specs=[pl.BlockSpec(memory_space=pltpu.SMEM)]
        + [pl.BlockSpec((h, CHUNK), lambda i: (0, first(i))) for h in heights]
        + [pl.BlockSpec((h, CHUNK), lambda i: (0, held(i))) for h in heights]
        + [
            pl.BlockSpec((hid, CHUNK), lambda i: (0, first(i))),
            pl.BlockSpec((CHUNK, hid), lambda i: (held(i), 0)),
            pl.BlockSpec((CHUNK, hid), lambda i: (held(i), 0)),
            pl.BlockSpec((rows, hid), fixed),
            pl.BlockSpec((rows, hid), fixed),
            pl.BlockSpec((rows, META), fixed),
        ],
        out_specs=[
            pl.BlockSpec((rows, CHUNK), lambda i: (0, first(i))),
            pl.BlockSpec((rows, 2 * hid), fixed),
        ]
        + [pl.BlockSpec((size, CHUNK), lambda i: (0, later(i)))] * (CORES * n3),
        out_shape=shapes,
        scratch_shapes=[
            pltpu.VMEM((rows, hid), jnp.float32),
            pltpu.VMEM((rows, hid), jnp.bfloat16),
            pltpu.VMEM((rows, hid), jnp.bfloat16),
            pltpu.VMEM((width // META + 8, META), jnp.float32),
        ],
        compiler_params=params(),
        cost_estimate=cost(6 * rows * width * hid, 6 * width * hid + 6 * rows * width),
        name="backward",
    )(spot, *grad, *tok, wd, wg, wu, pre_gate, pre_up, side)
    parts = [outs[2 + c * n3 : 2 + (c + 1) * n3] for c in range(CORES)]
    return outs[0], outs[1], parts


def up_grads(scaled, pre_grads):
    rows, width = scaled.shape
    hid = pre_grads.shape[1] // 2
    step = WIDE if rows <= WHOLE_ROWS else CHUNK
    return pl.pallas_call(
        up_grads_kernel,
        grid=(width // step,),
        in_specs=[
            pl.BlockSpec((rows, step), lambda i: (0, i)),
            pl.BlockSpec((rows, 2 * hid), lambda i: (0, 0)),
        ],
        out_specs=[pl.BlockSpec((step, hid), lambda i: (i, 0))] * 2,
        out_shape=[jax.ShapeDtypeStruct((width, hid), jnp.bfloat16)] * 2,
        compiler_params=params(20),
        cost_estimate=cost(4 * rows * width * hid, 4 * width * hid + 2 * rows * width),
        name="up_grads",
    )(*(on_chip(scaled, pre_grads) if rows <= WHOLE_ROWS else (scaled, pre_grads)))


def down_grad(hidden, og_all):
    rows, width = og_all.shape
    hid = hidden.shape[1]
    step = WIDE if rows <= WHOLE_ROWS else CHUNK
    return pl.pallas_call(
        down_grad_kernel,
        grid=(width // step,),
        in_specs=[
            pl.BlockSpec((rows, hid), lambda i: (0, 0)),
            pl.BlockSpec((rows, step), lambda i: (0, i)),
        ],
        out_specs=pl.BlockSpec((hid, step), lambda i: (0, i)),
        out_shape=jax.ShapeDtypeStruct((hid, width), jnp.bfloat16),
        compiler_params=params(20),
        cost_estimate=cost(2 * rows * width * hid, 2 * width * hid + 2 * rows * width),
        name="down_grad",
    )(*(on_chip(hidden, og_all) if rows <= WHOLE_ROWS else (hidden, og_all)))


def layer(tokens, out_grad, routes, gate_fixed, ramp_step, norm_gain, w_gate, w_up, w_down):
    seq_count = lax.axis_size("seq")
    ep_count = lax.axis_size("ep")
    torus = Torus(seq_count, ep_count)
    torus.check()
    width = tokens.shape[1]
    top = routes.shape[1]
    tok = gather(torus, pack(tokens, routes, gate_fixed))
    grad = gather(torus, out_grad)
    expert = lax.axis_index("ep")
    span = width // torus.count
    device = lax.axis_index("seq") * ep_count + expert
    start = (device * span % META).astype(jnp.uint32)
    spot = jnp.stack([expert.astype(jnp.uint32), device.astype(jnp.uint32), start])
    gain = norm_gain[None, :]
    wg, wu, wd = w_gate[0], w_up[0], w_down[0]
    if tokens.shape[0] * seq_count * ep_count <= WHOLE_ROWS:
        held = []
        for weight in (wg, wu, wd):
            held += prefetch(spot, [weight])
        wg, wu, wd = held
    scaled, pre_gate, pre_up, hidden, side, out_parts = forward(
        torus, tok, gain, wg, wu, wd, spot, ramp_step, top
    )
    og_all, pre_grads, parts = backward(torus, spot, grad, tok, wd, wg, wu, pre_gate, pre_up, side)
    w_gate_grad, w_up_grad = up_grads(scaled, pre_grads)
    mixed, w_gate_grad = scatter_sum(torus, out_parts, w_gate_grad)
    mixed = mixed.astype(jnp.bfloat16)
    total = scatter_sum(torus, parts)
    normed_grad = total[:, :width]
    count = gain_rows(span)
    gain_part = total[:count, width:] + total[count : 2 * count, width:]
    gain_grad = lax.dynamic_slice(gain_part.reshape(-1), (start,), (span,))
    w_down_grad = down_grad(hidden, og_all)[None]
    own = tokens.astype(jnp.float32)
    own_recip = lax.rsqrt(jnp.mean(own * own, axis=1, keepdims=True) + norm_eps)
    weighted = gain * normed_grad
    inner = jnp.sum(weighted * own, axis=1, keepdims=True)
    tokens_grad = (
        own_recip * weighted - own * own_recip * own_recip * own_recip * inner / width
    ).astype(jnp.bfloat16)
    return (mixed, tokens_grad, gain_grad, w_gate_grad[None], w_up_grad[None], w_down_grad)


def solution(mesh):
    return jax.shard_map(
        layer,
        mesh=mesh,
        in_specs=(
            P(("seq", "ep"), None),
            P(("seq", "ep"), None),
            P(("seq", "ep"), None),
            P(("seq", "ep"), None),
            P(),
            P(),
            P("ep", None, "seq"),
            P("ep", None, "seq"),
            P("ep", "seq", None),
        ),
        out_specs=(
            P(("seq", "ep"), None),
            P(("seq", "ep"), None),
            P(("seq", "ep")),
            P("ep", None, "seq"),
            P("ep", None, "seq"),
            P("ep", "seq", None),
        ),
        check_vma=False,
    )
```

```python
import functools

import jax
import jax.numpy as jnp
from jax import lax
from jax.experimental import pallas as pl
from jax.experimental.pallas import tpu as pltpu
from jax.sharding import PartitionSpec as P


RAMP = 8
CORES = 2
DEPTH = 4

gate_unit = 65536.0
norm_eps = 1e-06
META = 128
CHUNK = 1024
WIDE = 1792
WHOLE_ROWS = 256


AXES = ("seq", "ep")


def contract_rows(left, right):
    return lax.dot_general(
        left, right, (((0,), (0,)), ((), ())), preferred_element_type=jnp.float32
    )


def contract_cols(left, right):
    return lax.dot_general(
        left, right, (((1,), (1,)), ((), ())), preferred_element_type=jnp.float32
    )


def matmul(left, right):
    return jnp.dot(left, right, preferred_element_type=jnp.float32)


class Torus:
    def __init__(self, seq_count, ep_count):
        self.nx = seq_count
        self.nc = CORES
        self.nz = DEPTH
        self.ny = ep_count // (CORES * DEPTH)
        self.count = seq_count * ep_count
        self.swap = self.nx == self.ny

    def place(self, i):
        core = i % self.nc
        y = i // self.nc % self.ny
        z = i // (self.nc * self.ny) % self.nz
        x = i // (self.nc * self.ny * self.nz)
        return [x, z, y, core]

    def index(self, x, z, y, core):
        return ((x * self.nz + z) * self.ny + y) * self.nc + core

    def axis(self, step, core):
        first = 0 if (self.swap and core == 1) else 2
        return (1, first, 2 - first, 3)[step]

    def size(self, step):
        return (self.nz, self.ny, self.nx, self.nc)[step]

    def pairs(self, step, shift):
        sizes = [self.nx, self.nz, self.ny, self.nc]
        found = []
        for i in range(self.count):
            spot = self.place(i)
            axis = self.axis(step, spot[3])
            spot[axis] ^= shift
            found.append((i, self.index(*spot)))
        return found

    def check(self):
        assert all(n & (n - 1) == 0 for n in (self.nx, self.ny, self.nz, self.nc))


def shift_rows(torus, rows, step, shift):
    return lax.ppermute(rows, AXES, torus.pairs(step, shift))


def planes(torus, rows):
    second = [rows] + [shift_rows(torus, rows, 1, s) for s in range(1, torus.size(1))]
    third = [second] + [
        [shift_rows(torus, piece, 2, s) for piece in second]
        for s in range(1, torus.size(2))
    ]
    return [piece for row in third for piece in row]


def gather(torus, rows):
    near = jnp.concatenate(planes(torus, rows), axis=0)
    near_pair = shift_rows(torus, near, 3, 1)
    others = [shift_rows(torus, rows, 0, s) for s in range(1, torus.nz)]
    line = join(others)
    far = planes(torus, line)
    far_pair = [shift_rows(torus, piece, 3, 1) for piece in far]
    return far + far_pair + [near, near_pair]


def join_kernel(*refs):
    out = refs[-1]
    each = refs[0].shape[0]
    for k, ref in enumerate(refs[:-1]):
        out[k * each : (k + 1) * each, :] = ref[...]


def join(blocks):
    rows, width = blocks[0].shape
    vmem = pl.BlockSpec(memory_space=pltpu.VMEM)
    return pl.pallas_call(
        join_kernel,
        in_specs=[vmem] * len(blocks),
        out_specs=vmem,
        out_shape=jax.ShapeDtypeStruct((rows * len(blocks), width), blocks[0].dtype),
        compiler_params=limit(4),
        name="join",
    )(*blocks)


def load_rows(refs, cols):
    far, near = refs[:-2], refs[-2:]
    half = len(far) // CORES
    own = near[0].shape[0] // half
    found = []
    for core in range(CORES):
        block = near[core][:, cols].astype(jnp.float32)
        for k in range(half):
            wide = far[core * half + k][:, cols].astype(jnp.float32)
            found.append(jnp.concatenate([wide, block[k * own : (k + 1) * own]], axis=0))
    return found


def wide_sum(parts):
    total = parts[0].astype(jnp.float32)
    for part in parts[1:]:
        total = total + part.astype(jnp.float32)
    return total


def scatter_sum(torus, parts, after=None):
    n3, n2 = torus.size(2), torus.size(1)
    each = parts[0][0].shape[0] // n2
    got = [None] * n3
    for s3 in reversed(range(n3)):
        got[s3] = shift_rows(torus, parts[1][s3], 3, 1)
    near = [
        [
            [parts[0][s3][s2 * each : (s2 + 1) * each], got[s3][s2 * each : (s2 + 1) * each]]
            for s2 in range(n2)
        ]
        for s3 in range(n3)
    ]
    for s2 in reversed(range(n2)):
        for s3 in range(1, n3):
            send = wide_sum(near[s3][s2]).astype(jnp.bfloat16)
            near[0][s2].append(shift_rows(torus, send, 2, s3))
    for s2 in range(1, n2):
        send = wide_sum(near[0][s2]).astype(jnp.bfloat16)
        near[0][0].append(shift_rows(torus, send, 1, s2))
    if after is not None:
        near[0][0][-1], after = lax.optimization_barrier((near[0][0][-1], after))
    total = wide_sum(near[0][0])
    rows = each // torus.nz
    last = [total[each - rows :]]
    for shift in reversed(range(1, torus.nz)):
        block = total[(shift - 1) * rows : shift * rows].astype(jnp.bfloat16)
        last.append(shift_rows(torus, block, 0, shift))
    return wide_sum(last) if after is None else (wide_sum(last), after)


def gain_rows(span):
    return (span + 2 * META - 2) // META


def gain_tiles(torus, device, gain_ref, span, rows):
    count = gain_rows(span)
    core = device % CORES
    tiles = []
    for other in range(CORES):
        odd = (core + other) % CORES
        for s3 in range(torus.size(2)):
            for s2 in range(torus.size(1)):
                for sz in [*range(1, torus.nz), 0]:
                    even_mask = torus.index(s3, sz, s2, other)
                    odd_mask = torus.index(s2, sz, s3, other) if torus.swap else even_mask
                    target = device ^ jnp.where(odd == 1, odd_mask, even_mask)
                    value = gain_ref[pl.ds(target * span // META, count), :]
                    high = value.astype(jnp.bfloat16).astype(jnp.float32)
                    rest = jnp.zeros((rows - 2 * count, META), jnp.float32)
                    tiles.append(jnp.concatenate([high, value - high, rest], axis=0))
    return tiles


def gates_of(table, place, ramp_step, top):
    place = place.astype(jnp.int32)
    expert = place.astype(jnp.float32)
    ramp = ramp_step[place].astype(jnp.float32)
    gates = table[:, top : 2 * top] * 256.0 + table[:, 2 * top : 3 * top]
    coef = jnp.sum(jnp.where(table[:, :top] == expert, gates, 0.0), axis=1, keepdims=True)
    return coef / gate_unit * ramp / RAMP


def fold_lanes(rows):
    part = rows[:, :META]
    for c in range(1, rows.shape[1] // META):
        part = part + rows[:, c * META : (c + 1) * META]
    return part


def pack_kernel(tokens, routes, gates, out, meta):
    width = tokens.shape[1]
    top = routes.shape[1]
    out[:, :width] = tokens[...]
    fixed = gates[...]
    high = fixed // 256
    meta[...] = jnp.zeros_like(meta)
    meta[:, :top] = routes[...].astype(jnp.float32)
    meta[:, top : 2 * top] = high.astype(jnp.float32)
    meta[:, 2 * top : 3 * top] = (fixed - 256 * high).astype(jnp.float32)
    out[:, width:] = meta[...].astype(jnp.bfloat16)


def pack(tokens, routes, gates):
    rows, width = tokens.shape
    vmem = pl.BlockSpec(memory_space=pltpu.VMEM)
    return pl.pallas_call(
        pack_kernel,
        in_specs=[vmem] * 3,
        out_specs=vmem,
        out_shape=jax.ShapeDtypeStruct((rows, width + META), jnp.bfloat16),
        scratch_shapes=[pltpu.VMEM((rows, META), jnp.float32)],
        compiler_params=pltpu.CompilerParams(vmem_limit_bytes=4 * 2**20),
        name="pack",
    )(*off_chip(tokens, routes, gates))


def send_parts(rows, parts, cols, sems, first):
    size = parts[0].shape[0]
    copies = [
        pltpu.make_async_copy(
            rows.at[p * size : (p + 1) * size, cols], ref.at[:, cols], sems.at[first + p]
        )
        for p, ref in enumerate(parts)
    ]
    for copy in copies:
        copy.start()
    return copies


def forward_whole(*refs, pieces, width, top):
    spot, ramp_step = refs[:2]
    tok = refs[2 : 2 + pieces]
    gain, wg, wu = refs[2 + pieces : 5 + pieces]
    outs = refs[5 + pieces :]
    scaled, pre_gate, pre_up, hidden, side, acc_g, acc_u = outs
    squares = []
    for k in range(width // WIDE):
        cols = slice(k * WIDE, (k + 1) * WIDE)
        g = gain[:, cols]
        for p, x in enumerate(load_rows(tok, cols)):
            each = x.shape[0]
            scaled[p * each : (p + 1) * each, cols] = (x * g).astype(jnp.bfloat16)
            part = fold_lanes(x * x)
            if k == 0:
                squares.append(part)
            else:
                squares[p] = squares[p] + part
        xs = scaled[:, cols]
        if k == 0:
            acc_g[...] = matmul(xs, wg[cols, :])
            acc_u[...] = matmul(xs, wu[cols, :])
        else:
            acc_g[...] += matmul(xs, wg[cols, :])
            acc_u[...] += matmul(xs, wu[cols, :])
    total = jnp.sum(jnp.concatenate(squares, axis=0), axis=1, keepdims=True)
    recip = lax.rsqrt(total / width + norm_eps)
    table = jnp.concatenate(load_rows(tok, slice(width, width + META)), axis=0)
    coef = gates_of(table, spot[0], ramp_step, top)
    pg = recip * acc_g[...]
    pu = recip * acc_u[...]
    pre_gate[...] = pg
    pre_up[...] = pu
    hidden[...] = (coef * (pg * jax.nn.sigmoid(pg) * pu)).astype(jnp.bfloat16)
    lane = lax.broadcasted_iota(jnp.int32, side.shape, 1)
    side[...] = jnp.where(lane == 0, recip, jnp.where(lane == 1, coef, 0.0))


def out_whole(hidden, wd, *refs):
    parts = refs[:-2]
    sums, sems = refs[-2:]
    pending = []
    for k in range(wd.shape[1] // WIDE):
        cols = slice(k * WIDE, (k + 1) * WIDE)
        sums[:, cols] = matmul(hidden[...], wd[:, cols]).astype(jnp.bfloat16)
        pending += send_parts(sums, parts, cols, sems, k * len(parts))
    for copy in pending:
        copy.wait()


def backward_whole(*refs, pieces, width, torus):
    spot = refs[0]
    grad = refs[1 : 1 + pieces]
    tok = refs[1 + pieces : 1 + 2 * pieces]
    wd, wg, wu, pre_gate, pre_up, side = refs[1 + 2 * pieces : 7 + 2 * pieces]
    outs = refs[7 + 2 * pieces :]
    og_all, pre_grads = outs[:2]
    parts = outs[2:-6]
    acc, gate_s, up_s, sums, gain_ref, sems = outs[-6:]
    pending = []
    steps = width // WIDE
    for k in range(steps):
        cols = slice(k * WIDE, (k + 1) * WIDE)
        for p, rows in enumerate(load_rows(grad, cols)):
            each = rows.shape[0]
            og_all[p * each : (p + 1) * each, cols] = rows.astype(jnp.bfloat16)
        got = contract_cols(og_all[:, cols], wd[:, cols])
        if k == 0:
            acc[...] = got
        else:
            acc[...] += got
    recip = side[:, 0:1]
    coef = side[:, 1:2]
    pre_grads_of(acc, pre_gate, pre_up, recip, coef, gate_s, up_s, pre_grads)
    gain_ref[...] = jnp.zeros_like(gain_ref)
    for k in range(steps):
        cols = slice(k * WIDE, (k + 1) * WIDE)
        back = contract_cols(gate_s[...], wg[cols, :]) + contract_cols(up_s[...], wu[cols, :])
        sums[:, cols] = back.astype(jnp.bfloat16)
        total = None
        for p, x in enumerate(load_rows(tok, cols)):
            each = x.shape[0]
            rows = slice(p * each, (p + 1) * each)
            part = back[rows] * (x * recip[rows])
            total = part if p == 0 else total + part
        keep_gain(gain_ref, total, k * WIDE // META)
        if k == steps - 1:
            sums[:, width:] = gain_block(torus, spot, gain_ref, width, recip.shape[0])
            cols = slice(k * WIDE, width + META)
        pending += send_parts(sums, parts, cols, sems, steps + k * len(parts))
    for copy in pending:
        copy.wait()


def keep_gain(gain_ref, total, first):
    row = jnp.sum(total, axis=0, keepdims=True)
    for c in range(row.shape[1] // META):
        gain_ref[first + c : first + c + 1, :] = row[:, c * META : (c + 1) * META]


def gain_block(torus, spot, gain_ref, width, rows):
    device = spot[1].astype(jnp.int32)
    tiles = gain_tiles(torus, device, gain_ref, width // torus.count, rows // torus.count)
    return jnp.concatenate(tiles, axis=0).astype(jnp.bfloat16)


def prefetch_kernel(_, *refs):
    count = len(refs) // 2
    sems = refs[-1]
    copies = [
        pltpu.make_async_copy(refs[k], refs[count + k], sems.at[k]) for k in range(count)
    ]
    for copy in copies:
        copy.start()
    for copy in copies:
        copy.wait()


def off_chip(*arrays):
    return [pltpu.with_memory_space_constraint(a, pltpu.HBM) for a in arrays]


def on_chip(*arrays):
    return [pltpu.with_memory_space_constraint(a, pltpu.VMEM) for a in arrays]


def prefetch(spot, weights):
    return pl.pallas_call(
        prefetch_kernel,
        in_specs=[pl.BlockSpec(memory_space=pltpu.SMEM)]
        + [pl.BlockSpec(memory_space=pltpu.HBM)] * len(weights),
        out_specs=[pl.BlockSpec(memory_space=pltpu.VMEM)] * len(weights),
        out_shape=[pltpu.VMEM(w.shape, w.dtype) for w in weights],
        scratch_shapes=[pltpu.SemaphoreType.DMA((len(weights),))],
        compiler_params=pltpu.CompilerParams(vmem_limit_bytes=2**20),
        name="prefetch",
    )(spot, *off_chip(*weights))


def pre_grads_of(acc, pre_gate, pre_up, recip, coef, gate_s, up_s, pre_grads):
    hidden_grad = coef * acc[...]
    pg = pre_gate[...]
    pu = pre_up[...]
    sigma = jax.nn.sigmoid(pg)
    gate_grad = hidden_grad * pu * sigma * (1.0 + pg * (1.0 - sigma))
    up_grad = hidden_grad * (pg * sigma)
    gate_s[...] = gate_grad.astype(jnp.bfloat16)
    up_s[...] = up_grad.astype(jnp.bfloat16)
    half = gate_grad.shape[1]
    pre_grads[:, :half] = (recip * gate_grad).astype(jnp.bfloat16)
    pre_grads[:, half:] = (recip * up_grad).astype(jnp.bfloat16)


def forward_kernel(*refs, pieces, steps, width, top):
    spot, ramp_step = refs[:2]
    tok = refs[2 : 2 + pieces]
    meta = refs[2 + pieces : 2 + 2 * pieces]
    gain, wg, wu, wd = refs[2 + 2 * pieces : 6 + 2 * pieces]
    outs = refs[6 + 2 * pieces :]
    scaled, pre_gate, pre_up, hidden, side = outs[:5]
    parts = outs[5:-3]
    acc_g, acc_u, squares = outs[-3:]
    i = pl.program_id(0)

    @pl.when(i < steps)
    def _():
        g = gain[...]
        for p, x in enumerate(load_rows(tok, slice(None))):
            each = x.shape[0]
            part_rows = slice(p * each, (p + 1) * each)
            scaled[part_rows, :] = (x * g).astype(jnp.bfloat16)
            part = fold_lanes(x * x)
            squares[part_rows, :] = jnp.where(i == 0, part, squares[part_rows, :] + part)
        xs = scaled[...]
        got_g = matmul(xs, wg[...])
        got_u = matmul(xs, wu[...])

        @pl.when(i == 0)
        def _():
            acc_g[...] = got_g
            acc_u[...] = got_u

        @pl.when(i > 0)
        def _():
            acc_g[...] += got_g
            acc_u[...] += got_u

    @pl.when(i == steps - 1)
    def _():
        recip = lax.rsqrt(jnp.sum(squares[...], axis=1, keepdims=True) / width + norm_eps)
        table = jnp.concatenate(load_rows(meta, slice(None)), axis=0)
        coef = gates_of(table, spot[0], ramp_step, top)
        pg = recip * acc_g[...]
        pu = recip * acc_u[...]
        pre_gate[...] = pg
        pre_up[...] = pu
        hidden[...] = (coef * (pg * jax.nn.sigmoid(pg) * pu)).astype(jnp.bfloat16)
        lane = lax.broadcasted_iota(jnp.int32, side.shape, 1)
        side[...] = jnp.where(lane == 0, recip, jnp.where(lane == 1, coef, 0.0))

    @pl.when(i >= steps)
    def _():
        out = matmul(hidden[...], wd[...]).astype(jnp.bfloat16)
        size = parts[0].shape[0]
        for p, ref in enumerate(parts):
            ref[...] = out[p * size : (p + 1) * size]


def backward_kernel(*refs, pieces, steps, width, torus):
    spot = refs[0]
    grad = refs[1 : 1 + pieces]
    tok = refs[1 + pieces : 1 + 2 * pieces]
    wd, wg, wu, pre_gate, pre_up, side = refs[1 + 2 * pieces : 7 + 2 * pieces]
    outs = refs[7 + 2 * pieces :]
    og_all, pre_grads = outs[:2]
    parts = outs[2:-4]
    acc, gate_s, up_s, gain_ref = outs[-4:]
    i = pl.program_id(0)
    size = parts[0].shape[0]

    @pl.when(i < steps)
    def _():
        for p, rows in enumerate(load_rows(grad, slice(None))):
            each = rows.shape[0]
            og_all[p * each : (p + 1) * each, :] = rows.astype(jnp.bfloat16)
        got = contract_cols(og_all[...], wd[...])

        @pl.when(i == 0)
        def _():
            acc[...] = got
            gain_ref[...] = jnp.zeros_like(gain_ref)

        @pl.when(i > 0)
        def _():
            acc[...] += got

    @pl.when(i == steps - 1)
    def _():
        recip = side[:, 0:1]
        coef = side[:, 1:2]
        pre_grads_of(acc, pre_gate, pre_up, recip, coef, gate_s, up_s, pre_grads)

    for k in range(steps):

        @pl.when(i == steps + k)
        def _(k=k):
            back = contract_cols(gate_s[...], wg[...]) + contract_cols(up_s[...], wu[...])
            recip = side[:, 0:1]
            total = None
            for p, x in enumerate(load_rows(tok, slice(None))):
                each = x.shape[0]
                rows = slice(p * each, (p + 1) * each)
                part = back[rows] * (x * recip[rows])
                total = part if p == 0 else total + part
            keep_gain(gain_ref, total, k * CHUNK // META)
            out = back.astype(jnp.bfloat16)
            for p, ref in enumerate(parts):
                ref[...] = out[p * size : (p + 1) * size]

    @pl.when(i == 2 * steps)
    def _():
        out = gain_block(torus, spot, gain_ref, width, side.shape[0])
        for p, ref in enumerate(parts):
            ref[:, :META] = out[p * size : (p + 1) * size]


def up_grads_kernel(scaled, pre_grads, wg_grad, wu_grad):
    both = contract_rows(scaled[...], pre_grads[...]).astype(jnp.bfloat16)
    half = wg_grad.shape[1]
    wg_grad[...] = both[:, :half]
    wu_grad[...] = both[:, half:]


def down_grad_kernel(hidden, og_all, wd_grad):
    wd_grad[...] = contract_rows(hidden[...], og_all[...]).astype(jnp.bfloat16)


def params(mib=56):
    return pltpu.CompilerParams(dimension_semantics=("arbitrary",), vmem_limit_bytes=mib * 2**20)


def placed(shapes, low, high):
    return [
        (pltpu.VMEM if low <= k < high else pltpu.HBM)(s.shape, s.dtype)
        for k, s in enumerate(shapes)
    ]


def shapes_of(rows, width, hid, size, parts):
    scratch = [
        jax.ShapeDtypeStruct((rows, width), jnp.bfloat16),
        jax.ShapeDtypeStruct((rows, hid), jnp.float32),
        jax.ShapeDtypeStruct((rows, hid), jnp.float32),
        jax.ShapeDtypeStruct((rows, hid), jnp.bfloat16),
        jax.ShapeDtypeStruct((rows, META), jnp.float32),
    ]
    return scratch + [jax.ShapeDtypeStruct((size, width), jnp.bfloat16)] * parts


def limit(mib):
    return pltpu.CompilerParams(vmem_limit_bytes=mib * 2**20)


def cost(flops, size):
    return pl.CostEstimate(flops=int(flops), bytes_accessed=int(size), transcendentals=0)


def forward(torus, tok, gain, wg, wu, wd, spot, ramp_step, top):
    width, hid = wg.shape
    steps = width // CHUNK
    pieces = len(tok)
    heights = [t.shape[0] for t in tok]
    rows = sum(heights)
    n3 = torus.size(2)
    size = rows // (CORES * n3)
    first = lambda i: jnp.minimum(i, steps - 1)
    later = lambda i: jnp.maximum(i - steps, 0)
    fixed = lambda i: (0, 0)
    if rows <= WHOLE_ROWS:
        vmem = pl.BlockSpec(memory_space=pltpu.VMEM)
        hbm = pl.BlockSpec(memory_space=pltpu.HBM)
        shapes = shapes_of(rows, width, hid, size, CORES * n3)
        outs = pl.pallas_call(
            functools.partial(forward_whole, pieces=pieces, width=width, top=top),
            in_specs=[pl.BlockSpec(memory_space=pltpu.SMEM)] * 2 + [vmem] * (pieces + 3),
            out_specs=[vmem] * 5,
            out_shape=placed(shapes[:5], 0, 5),
            scratch_shapes=[pltpu.VMEM((rows, hid), jnp.float32)] * 2,
            compiler_params=limit(8),
            cost_estimate=cost(4 * rows * width * hid, 4 * width * hid + 4 * rows * width),
            name="forward",
        )(spot, ramp_step, *tok, gain, *on_chip(wg, wu))
        parts = pl.pallas_call(
            out_whole,
            in_specs=[vmem] * 2,
            out_specs=[hbm] * (CORES * n3),
            out_shape=placed(shapes[5:], 0, 0),
            scratch_shapes=[
                pltpu.VMEM((rows, width), jnp.bfloat16),
                pltpu.SemaphoreType.DMA((width // WIDE * CORES * n3,)),
            ],
            compiler_params=limit(6),
            cost_estimate=cost(2 * rows * width * hid, 2 * width * hid + 2 * rows * width),
            name="out",
        )(*on_chip(outs[3], wd))
        return (*outs, [parts[c * n3 : (c + 1) * n3] for c in range(CORES)])
    outs = pl.pallas_call(
        functools.partial(forward_kernel, pieces=pieces, steps=steps, width=width, top=top),
        grid=(2 * steps,),
        in_specs=[pl.BlockSpec(memory_space=pltpu.SMEM)] * 2
        + [pl.BlockSpec((h, CHUNK), lambda i: (0, first(i))) for h in heights]
        + [pl.BlockSpec((h, META), lambda i: (0, width // META)) for h in heights]
        + [
            pl.BlockSpec((1, CHUNK), lambda i: (0, first(i))),
            pl.BlockSpec((CHUNK, hid), lambda i: (first(i), 0)),
            pl.BlockSpec((CHUNK, hid), lambda i: (first(i), 0)),
            pl.BlockSpec((hid, CHUNK), lambda i: (0, later(i))),
        ],
        out_specs=[
            pl.BlockSpec((rows, CHUNK), lambda i: (0, first(i))),
            pl.BlockSpec((rows, hid), fixed),
            pl.BlockSpec((rows, hid), fixed),
            pl.BlockSpec((rows, hid), fixed),
            pl.BlockSpec((rows, META), fixed),
        ]
        + [pl.BlockSpec((size, CHUNK), lambda i: (0, later(i)))] * (CORES * n3),
        out_shape=shapes_of(rows, width, hid, size, CORES * n3),
        scratch_shapes=[
            pltpu.VMEM((rows, hid), jnp.float32),
            pltpu.VMEM((rows, hid), jnp.float32),
            pltpu.VMEM((rows, META), jnp.float32),
        ],
        compiler_params=params(),
        cost_estimate=cost(6 * rows * width * hid, 6 * width * hid + 6 * rows * width),
        name="forward",
    )(spot, ramp_step, *tok, *tok, gain, wg, wu, wd)
    scaled, pre_gate, pre_up, hidden, side = outs[:5]
    parts = [outs[5 + c * n3 : 5 + (c + 1) * n3] for c in range(CORES)]
    return scaled, pre_gate, pre_up, hidden, side, parts


def backward(torus, spot, grad, tok, wd, wg, wu, pre_gate, pre_up, side):
    width, hid = wg.shape
    steps = width // CHUNK
    pieces = len(grad)
    heights = [g.shape[0] for g in grad]
    rows = sum(heights)
    n3 = torus.size(2)
    size = rows // (CORES * n3)
    first = lambda i: jnp.minimum(i, steps - 1)
    later = lambda i: jnp.maximum(i - steps, 0)
    held = lambda i: jnp.clip(i - steps, 0, steps - 1)
    fixed = lambda i: (0, 0)
    shapes = [
        jax.ShapeDtypeStruct((rows, width), jnp.bfloat16),
        jax.ShapeDtypeStruct((rows, 2 * hid), jnp.bfloat16),
    ] + [jax.ShapeDtypeStruct((size, width + META), jnp.bfloat16)] * (CORES * n3)
    if rows <= WHOLE_ROWS:
        vmem = pl.BlockSpec(memory_space=pltpu.VMEM)
        hbm = pl.BlockSpec(memory_space=pltpu.HBM)
        outs = pl.pallas_call(
            functools.partial(backward_whole, pieces=pieces, width=width, torus=torus),
            in_specs=[pl.BlockSpec(memory_space=pltpu.SMEM)] + [vmem] * (2 * pieces + 6),
            out_specs=[vmem, vmem] + [hbm] * (CORES * n3),
            out_shape=placed(shapes, 0, 2),
            scratch_shapes=[
                pltpu.VMEM((rows, hid), jnp.float32),
                pltpu.VMEM((rows, hid), jnp.bfloat16),
                pltpu.VMEM((rows, hid), jnp.bfloat16),
                pltpu.VMEM((rows, width + META), jnp.bfloat16),
                pltpu.VMEM((width // META + 8, META), jnp.float32),
                pltpu.SemaphoreType.DMA((width // WIDE * (1 + CORES * n3),)),
            ],
            compiler_params=limit(12),
            cost_estimate=cost(6 * rows * width * hid, 6 * width * hid + 6 * rows * width),
            name="backward",
        )(spot, *grad, *tok, *on_chip(wd, wg, wu, pre_gate, pre_up, side))
        return (*outs[:2], [outs[2 + c * n3 : 2 + (c + 1) * n3] for c in range(CORES)])
    outs = pl.pallas_call(
        functools.partial(backward_kernel, pieces=pieces, steps=steps, width=width, torus=torus),
        grid=(2 * steps + 1,),
        in_specs=[pl.BlockSpec(memory_space=pltpu.SMEM)]
        + [pl.BlockSpec((h, CHUNK), lambda i: (0, first(i))) for h in heights]
        + [pl.BlockSpec((h, CHUNK), lambda i: (0, held(i))) for h in heights]
        + [
            pl.BlockSpec((hid, CHUNK), lambda i: (0, first(i))),
            pl.BlockSpec((CHUNK, hid), lambda i: (held(i), 0)),
            pl.BlockSpec((CHUNK, hid), lambda i: (held(i), 0)),
            pl.BlockSpec((rows, hid), fixed),
            pl.BlockSpec((rows, hid), fixed),
            pl.BlockSpec((rows, META), fixed),
        ],
        out_specs=[
            pl.BlockSpec((rows, CHUNK), lambda i: (0, first(i))),
            pl.BlockSpec((rows, 2 * hid), fixed),
        ]
        + [pl.BlockSpec((size, CHUNK), lambda i: (0, later(i)))] * (CORES * n3),
        out_shape=shapes,
        scratch_shapes=[
            pltpu.VMEM((rows, hid), jnp.float32),
            pltpu.VMEM((rows, hid), jnp.bfloat16),
            pltpu.VMEM((rows, hid), jnp.bfloat16),
            pltpu.VMEM((width // META + 8, META), jnp.float32),
        ],
        compiler_params=params(),
        cost_estimate=cost(6 * rows * width * hid, 6 * width * hid + 6 * rows * width),
        name="backward",
    )(spot, *grad, *tok, wd, wg, wu, pre_gate, pre_up, side)
    parts = [outs[2 + c * n3 : 2 + (c + 1) * n3] for c in range(CORES)]
    return outs[0], outs[1], parts


def up_grads(scaled, pre_grads):
    rows, width = scaled.shape
    hid = pre_grads.shape[1] // 2
    step = WIDE if rows <= WHOLE_ROWS else CHUNK
    return pl.pallas_call(
        up_grads_kernel,
        grid=(width // step,),
        in_specs=[
            pl.BlockSpec((rows, step), lambda i: (0, i)),
            pl.BlockSpec((rows, 2 * hid), lambda i: (0, 0)),
        ],
        out_specs=[pl.BlockSpec((step, hid), lambda i: (i, 0))] * 2,
        out_shape=[jax.ShapeDtypeStruct((width, hid), jnp.bfloat16)] * 2,
        compiler_params=params(20),
        cost_estimate=cost(4 * rows * width * hid, 4 * width * hid + 2 * rows * width),
        name="up_grads",
    )(*(on_chip(scaled, pre_grads) if rows <= WHOLE_ROWS else (scaled, pre_grads)))


def down_grad(hidden, og_all):
    rows, width = og_all.shape
    hid = hidden.shape[1]
    step = WIDE if rows <= WHOLE_ROWS else CHUNK
    return pl.pallas_call(
        down_grad_kernel,
        grid=(width // step,),
        in_specs=[
            pl.BlockSpec((rows, hid), lambda i: (0, 0)),
            pl.BlockSpec((rows, step), lambda i: (0, i)),
        ],
        out_specs=pl.BlockSpec((hid, step), lambda i: (0, i)),
        out_shape=jax.ShapeDtypeStruct((hid, width), jnp.bfloat16),
        compiler_params=params(20),
        cost_estimate=cost(2 * rows * width * hid, 2 * width * hid + 2 * rows * width),
        name="down_grad",
    )(*(on_chip(hidden, og_all) if rows <= WHOLE_ROWS else (hidden, og_all)))


def layer(tokens, out_grad, routes, gate_fixed, ramp_step, norm_gain, w_gate, w_up, w_down):
    seq_count = lax.axis_size("seq")
    ep_count = lax.axis_size("ep")
    torus = Torus(seq_count, ep_count)
    torus.check()
    width = tokens.shape[1]
    top = routes.shape[1]
    tok = gather(torus, pack(tokens, routes, gate_fixed))
    grad = gather(torus, out_grad)
    expert = lax.axis_index("ep")
    span = width // torus.count
    device = lax.axis_index("seq") * ep_count + expert
    start = (device * span % META).astype(jnp.uint32)
    spot = jnp.stack([expert.astype(jnp.uint32), device.astype(jnp.uint32), start])
    gain = norm_gain[None, :]
    wg, wu, wd = w_gate[0], w_up[0], w_down[0]
    if tokens.shape[0] * seq_count * ep_count <= WHOLE_ROWS:
        held = []
        for weight in (wg, wu):
            held += prefetch(spot, [weight])
        wg, wu = held
    scaled, pre_gate, pre_up, hidden, side, out_parts = forward(
        torus, tok, gain, wg, wu, wd, spot, ramp_step, top
    )
    og_all, pre_grads, parts = backward(torus, spot, grad, tok, wd, wg, wu, pre_gate, pre_up, side)
    w_gate_grad, w_up_grad = up_grads(scaled, pre_grads)
    w_down_grad = down_grad(hidden, og_all)
    mixed, w_down_grad = scatter_sum(torus, out_parts, w_down_grad)
    mixed = mixed.astype(jnp.bfloat16)
    total = scatter_sum(torus, parts)
    normed_grad = total[:, :width]
    count = gain_rows(span)
    gain_part = total[:count, width:] + total[count : 2 * count, width:]
    gain_grad = lax.dynamic_slice(gain_part.reshape(-1), (start,), (span,))
    own = tokens.astype(jnp.float32)
    own_recip = lax.rsqrt(jnp.mean(own * own, axis=1, keepdims=True) + norm_eps)
    weighted = gain * normed_grad
    inner = jnp.sum(weighted * own, axis=1, keepdims=True)
    tokens_grad = (
        own_recip * weighted - own * own_recip * own_recip * own_recip * inner / width
    ).astype(jnp.bfloat16)
    return (mixed, tokens_grad, gain_grad, w_gate_grad[None], w_up_grad[None], w_down_grad[None])


def solution(mesh):
    return jax.shard_map(
        layer,
        mesh=mesh,
        in_specs=(
            P(("seq", "ep"), None),
            P(("seq", "ep"), None),
            P(("seq", "ep"), None),
            P(("seq", "ep"), None),
            P(),
            P(),
            P("ep", None, "seq"),
            P("ep", None, "seq"),
            P("ep", "seq", None),
        ),
        out_specs=(
            P(("seq", "ep"), None),
            P(("seq", "ep"), None),
            P(("seq", "ep")),
            P("ep", None, "seq"),
            P("ep", None, "seq"),
            P("ep", "seq", None),
        ),
        check_vma=False,
    )
```

```python
import functools

import jax
import jax.numpy as jnp
from jax import lax
from jax.experimental import pallas as pl
from jax.experimental.pallas import tpu as pltpu
from jax.sharding import PartitionSpec as P


RAMP = 8
CORES = 2
DEPTH = 4

gate_unit = 65536.0
norm_eps = 1e-06
META = 128
CHUNK = 1024
WIDE = 1792
WHOLE_ROWS = 256


AXES = ("seq", "ep")


def contract_rows(left, right):
    return lax.dot_general(
        left, right, (((0,), (0,)), ((), ())), preferred_element_type=jnp.float32
    )


def contract_cols(left, right):
    return lax.dot_general(
        left, right, (((1,), (1,)), ((), ())), preferred_element_type=jnp.float32
    )


def matmul(left, right):
    return jnp.dot(left, right, preferred_element_type=jnp.float32)


class Torus:
    def __init__(self, seq_count, ep_count):
        self.nx = seq_count
        self.nc = CORES
        self.nz = DEPTH
        self.ny = ep_count // (CORES * DEPTH)
        self.count = seq_count * ep_count
        self.swap = self.nx == self.ny

    def place(self, i):
        core = i % self.nc
        y = i // self.nc % self.ny
        z = i // (self.nc * self.ny) % self.nz
        x = i // (self.nc * self.ny * self.nz)
        return [x, z, y, core]

    def index(self, x, z, y, core):
        return ((x * self.nz + z) * self.ny + y) * self.nc + core

    def axis(self, step, core):
        first = 0 if (self.swap and core == 1) else 2
        return (1, first, 2 - first, 3)[step]

    def size(self, step):
        return (self.nz, self.ny, self.nx, self.nc)[step]

    def pairs(self, step, shift):
        sizes = [self.nx, self.nz, self.ny, self.nc]
        found = []
        for i in range(self.count):
            spot = self.place(i)
            axis = self.axis(step, spot[3])
            spot[axis] ^= shift
            found.append((i, self.index(*spot)))
        return found

    def check(self):
        assert all(n & (n - 1) == 0 for n in (self.nx, self.ny, self.nz, self.nc))


def shift_rows(torus, rows, step, shift):
    return lax.ppermute(rows, AXES, torus.pairs(step, shift))


def planes(torus, rows):
    second = [rows] + [shift_rows(torus, rows, 1, s) for s in range(1, torus.size(1))]
    third = [second] + [
        [shift_rows(torus, piece, 2, s) for piece in second]
        for s in range(1, torus.size(2))
    ]
    return [piece for row in third for piece in row]


def gather(torus, rows):
    near = jnp.concatenate(planes(torus, rows), axis=0)
    near_pair = shift_rows(torus, near, 3, 1)
    others = [shift_rows(torus, rows, 0, s) for s in range(1, torus.nz)]
    line = join(others)
    far = planes(torus, line)
    far_pair = [shift_rows(torus, piece, 3, 1) for piece in far]
    return far + far_pair + [near, near_pair]


def join_kernel(*refs):
    out = refs[-1]
    each = refs[0].shape[0]
    for k, ref in enumerate(refs[:-1]):
        out[k * each : (k + 1) * each, :] = ref[...]


def join(blocks):
    rows, width = blocks[0].shape
    vmem = pl.BlockSpec(memory_space=pltpu.VMEM)
    return pl.pallas_call(
        join_kernel,
        in_specs=[vmem] * len(blocks),
        out_specs=vmem,
        out_shape=jax.ShapeDtypeStruct((rows * len(blocks), width), blocks[0].dtype),
        compiler_params=limit(4),
        name="join",
    )(*blocks)


def load_rows(refs, cols):
    far, near = refs[:-2], refs[-2:]
    half = len(far) // CORES
    own = near[0].shape[0] // half
    found = []
    for core in range(CORES):
        block = near[core][:, cols].astype(jnp.float32)
        for k in range(half):
            wide = far[core * half + k][:, cols].astype(jnp.float32)
            found.append(jnp.concatenate([wide, block[k * own : (k + 1) * own]], axis=0))
    return found


def wide_sum(parts):
    total = parts[0].astype(jnp.float32)
    for part in parts[1:]:
        total = total + part.astype(jnp.float32)
    return total


def scatter_sum(torus, parts, after=None):
    n3, n2 = torus.size(2), torus.size(1)
    each = parts[0][0].shape[0] // n2
    got = [None] * n3
    for s3 in reversed(range(n3)):
        got[s3] = shift_rows(torus, parts[1][s3], 3, 1)
    near = [
        [
            [parts[0][s3][s2 * each : (s2 + 1) * each], got[s3][s2 * each : (s2 + 1) * each]]
            for s2 in range(n2)
        ]
        for s3 in range(n3)
    ]
    for s2 in reversed(range(n2)):
        for s3 in range(1, n3):
            send = wide_sum(near[s3][s2]).astype(jnp.bfloat16)
            near[0][s2].append(shift_rows(torus, send, 2, s3))
    for s2 in range(1, n2):
        send = wide_sum(near[0][s2]).astype(jnp.bfloat16)
        near[0][0].append(shift_rows(torus, send, 1, s2))
    if after is not None:
        near[0][0][-1], after = lax.optimization_barrier((near[0][0][-1], after))
    total = wide_sum(near[0][0])
    rows = each // torus.nz
    last = [total[each - rows :]]
    for shift in reversed(range(1, torus.nz)):
        block = total[(shift - 1) * rows : shift * rows].astype(jnp.bfloat16)
        last.append(shift_rows(torus, block, 0, shift))
    return wide_sum(last) if after is None else (wide_sum(last), after)


def gain_rows(span):
    return (span + 2 * META - 2) // META


def gain_tiles(torus, device, gain_ref, span, rows):
    count = gain_rows(span)
    core = device % CORES
    tiles = []
    for other in range(CORES):
        odd = (core + other) % CORES
        for s3 in range(torus.size(2)):
            for s2 in range(torus.size(1)):
                for sz in [*range(1, torus.nz), 0]:
                    even_mask = torus.index(s3, sz, s2, other)
                    odd_mask = torus.index(s2, sz, s3, other) if torus.swap else even_mask
                    target = device ^ jnp.where(odd == 1, odd_mask, even_mask)
                    value = gain_ref[pl.ds(target * span // META, count), :]
                    high = value.astype(jnp.bfloat16).astype(jnp.float32)
                    rest = jnp.zeros((rows - 2 * count, META), jnp.float32)
                    tiles.append(jnp.concatenate([high, value - high, rest], axis=0))
    return tiles


def gates_of(table, place, ramp_step, top):
    place = place.astype(jnp.int32)
    expert = place.astype(jnp.float32)
    ramp = ramp_step[place].astype(jnp.float32)
    gates = table[:, top : 2 * top] * 256.0 + table[:, 2 * top : 3 * top]
    coef = jnp.sum(jnp.where(table[:, :top] == expert, gates, 0.0), axis=1, keepdims=True)
    return coef / gate_unit * ramp / RAMP


def fold_lanes(rows):
    part = rows[:, :META]
    for c in range(1, rows.shape[1] // META):
        part = part + rows[:, c * META : (c + 1) * META]
    return part


def pack_kernel(tokens, routes, gates, out, meta):
    width = tokens.shape[1]
    top = routes.shape[1]
    out[:, :width] = tokens[...]
    fixed = gates[...]
    high = fixed // 256
    meta[...] = jnp.zeros_like(meta)
    meta[:, :top] = routes[...].astype(jnp.float32)
    meta[:, top : 2 * top] = high.astype(jnp.float32)
    meta[:, 2 * top : 3 * top] = (fixed - 256 * high).astype(jnp.float32)
    out[:, width:] = meta[...].astype(jnp.bfloat16)


def pack(tokens, routes, gates):
    rows, width = tokens.shape
    vmem = pl.BlockSpec(memory_space=pltpu.VMEM)
    return pl.pallas_call(
        pack_kernel,
        in_specs=[vmem] * 3,
        out_specs=vmem,
        out_shape=jax.ShapeDtypeStruct((rows, width + META), jnp.bfloat16),
        scratch_shapes=[pltpu.VMEM((rows, META), jnp.float32)],
        compiler_params=pltpu.CompilerParams(vmem_limit_bytes=4 * 2**20),
        name="pack",
    )(*off_chip(tokens, routes, gates))


def store_parts(parts, cols, rows):
    size = parts[0].shape[0]
    for p, ref in enumerate(parts):
        ref[:, cols] = rows[p * size : (p + 1) * size]


def forward_whole(*refs, pieces, width, top):
    spot, ramp_step = refs[:2]
    tok = refs[2 : 2 + pieces]
    gain, wg, wu = refs[2 + pieces : 5 + pieces]
    outs = refs[5 + pieces :]
    scaled_out, pre_gate, pre_up, hidden, side, acc_g, acc_u, scaled, sems = outs
    pending = []
    squares = []
    for k in range(width // WIDE):
        cols = slice(k * WIDE, (k + 1) * WIDE)
        g = gain[:, cols]
        for p, x in enumerate(load_rows(tok, cols)):
            each = x.shape[0]
            scaled[p * each : (p + 1) * each, cols] = (x * g).astype(jnp.bfloat16)
            part = fold_lanes(x * x)
            if k == 0:
                squares.append(part)
            else:
                squares[p] = squares[p] + part
        pending.append(pltpu.make_async_copy(scaled.at[:, cols], scaled_out.at[:, cols], sems.at[k]))
        pending[-1].start()
        xs = scaled[:, cols]
        if k == 0:
            acc_g[...] = matmul(xs, wg[cols, :])
            acc_u[...] = matmul(xs, wu[cols, :])
        else:
            acc_g[...] += matmul(xs, wg[cols, :])
            acc_u[...] += matmul(xs, wu[cols, :])
    total = jnp.sum(jnp.concatenate(squares, axis=0), axis=1, keepdims=True)
    recip = lax.rsqrt(total / width + norm_eps)
    table = jnp.concatenate(load_rows(tok, slice(width, width + META)), axis=0)
    coef = gates_of(table, spot[0], ramp_step, top)
    pg = recip * acc_g[...]
    pu = recip * acc_u[...]
    pre_gate[...] = pg
    pre_up[...] = pu
    hidden[...] = (coef * (pg * jax.nn.sigmoid(pg) * pu)).astype(jnp.bfloat16)
    lane = lax.broadcasted_iota(jnp.int32, side.shape, 1)
    side[...] = jnp.where(lane == 0, recip, jnp.where(lane == 1, coef, 0.0))
    for copy in pending:
        copy.wait()


def out_whole(hidden, wd, *parts):
    for k in range(wd.shape[1] // WIDE):
        cols = slice(k * WIDE, (k + 1) * WIDE)
        store_parts(parts, cols, matmul(hidden[...], wd[:, cols]).astype(jnp.bfloat16))


def backward_whole(*refs, pieces, width, torus):
    spot = refs[0]
    grad = refs[1 : 1 + pieces]
    tok = refs[1 + pieces : 1 + 2 * pieces]
    wd, wg, wu, pre_gate, pre_up, side = refs[1 + 2 * pieces : 7 + 2 * pieces]
    outs = refs[7 + 2 * pieces :]
    og_all, pre_grads = outs[:2]
    parts = outs[2:-6]
    acc, gate_s, up_s, gain_ref, wd_s, sems = outs[-6:]
    fetches = []
    for k in range(width // WIDE):
        cols = slice(k * WIDE, (k + 1) * WIDE)
        fetches.append(pltpu.make_async_copy(wd.at[:, cols], wd_s.at[:, cols], sems.at[k]))
        fetches[-1].start()
    steps = width // WIDE
    for k in range(steps):
        cols = slice(k * WIDE, (k + 1) * WIDE)
        for p, rows in enumerate(load_rows(grad, cols)):
            each = rows.shape[0]
            og_all[p * each : (p + 1) * each, cols] = rows.astype(jnp.bfloat16)
        fetches[k].wait()
        got = contract_cols(og_all[:, cols], wd_s[:, cols])
        if k == 0:
            acc[...] = got
        else:
            acc[...] += got
    recip = side[:, 0:1]
    coef = side[:, 1:2]
    pre_grads_of(acc, pre_gate, pre_up, recip, coef, gate_s, up_s, pre_grads)
    gain_ref[...] = jnp.zeros_like(gain_ref)
    for k in range(steps):
        cols = slice(k * WIDE, (k + 1) * WIDE)
        back = contract_cols(gate_s[...], wg[cols, :]) + contract_cols(up_s[...], wu[cols, :])
        store_parts(parts, cols, back.astype(jnp.bfloat16))
        total = None
        for p, x in enumerate(load_rows(tok, cols)):
            each = x.shape[0]
            rows = slice(p * each, (p + 1) * each)
            part = back[rows] * (x * recip[rows])
            total = part if p == 0 else total + part
        keep_gain(gain_ref, total, k * WIDE // META)
    block = gain_block(torus, spot, gain_ref, width, recip.shape[0])
    store_parts(parts, slice(width, width + META), block)


def keep_gain(gain_ref, total, first):
    row = jnp.sum(total, axis=0, keepdims=True)
    for c in range(row.shape[1] // META):
        gain_ref[first + c : first + c + 1, :] = row[:, c * META : (c + 1) * META]


def gain_block(torus, spot, gain_ref, width, rows):
    device = spot[1].astype(jnp.int32)
    tiles = gain_tiles(torus, device, gain_ref, width // torus.count, rows // torus.count)
    return jnp.concatenate(tiles, axis=0).astype(jnp.bfloat16)


def prefetch_kernel(_, *refs):
    count = len(refs) // 2
    sems = refs[-1]
    copies = [
        pltpu.make_async_copy(refs[k], refs[count + k], sems.at[k]) for k in range(count)
    ]
    for copy in copies:
        copy.start()
    for copy in copies:
        copy.wait()


def off_chip(*arrays):
    return [pltpu.with_memory_space_constraint(a, pltpu.HBM) for a in arrays]


def on_chip(*arrays):
    return [pltpu.with_memory_space_constraint(a, pltpu.VMEM) for a in arrays]


def prefetch(spot, weights):
    return pl.pallas_call(
        prefetch_kernel,
        in_specs=[pl.BlockSpec(memory_space=pltpu.SMEM)]
        + [pl.BlockSpec(memory_space=pltpu.HBM)] * len(weights),
        out_specs=[pl.BlockSpec(memory_space=pltpu.VMEM)] * len(weights),
        out_shape=[pltpu.VMEM(w.shape, w.dtype) for w in weights],
        scratch_shapes=[pltpu.SemaphoreType.DMA((len(weights),))],
        compiler_params=pltpu.CompilerParams(vmem_limit_bytes=2**20),
        name="prefetch",
    )(spot, *off_chip(*weights))


def pre_grads_of(acc, pre_gate, pre_up, recip, coef, gate_s, up_s, pre_grads):
    hidden_grad = coef * acc[...]
    pg = pre_gate[...]
    pu = pre_up[...]
    sigma = jax.nn.sigmoid(pg)
    gate_grad = hidden_grad * pu * sigma * (1.0 + pg * (1.0 - sigma))
    up_grad = hidden_grad * (pg * sigma)
    gate_s[...] = gate_grad.astype(jnp.bfloat16)
    up_s[...] = up_grad.astype(jnp.bfloat16)
    half = gate_grad.shape[1]
    pre_grads[:, :half] = (recip * gate_grad).astype(jnp.bfloat16)
    pre_grads[:, half:] = (recip * up_grad).astype(jnp.bfloat16)


def forward_kernel(*refs, pieces, steps, width, top):
    spot, ramp_step = refs[:2]
    tok = refs[2 : 2 + pieces]
    meta = refs[2 + pieces : 2 + 2 * pieces]
    gain, wg, wu, wd = refs[2 + 2 * pieces : 6 + 2 * pieces]
    outs = refs[6 + 2 * pieces :]
    scaled, pre_gate, pre_up, hidden, side = outs[:5]
    parts = outs[5:-3]
    acc_g, acc_u, squares = outs[-3:]
    i = pl.program_id(0)

    @pl.when(i < steps)
    def _():
        g = gain[...]
        for p, x in enumerate(load_rows(tok, slice(None))):
            each = x.shape[0]
            part_rows = slice(p * each, (p + 1) * each)
            scaled[part_rows, :] = (x * g).astype(jnp.bfloat16)
            part = fold_lanes(x * x)
            squares[part_rows, :] = jnp.where(i == 0, part, squares[part_rows, :] + part)
        xs = scaled[...]
        got_g = matmul(xs, wg[...])
        got_u = matmul(xs, wu[...])

        @pl.when(i == 0)
        def _():
            acc_g[...] = got_g
            acc_u[...] = got_u

        @pl.when(i > 0)
        def _():
            acc_g[...] += got_g
            acc_u[...] += got_u

    @pl.when(i == steps - 1)
    def _():
        recip = lax.rsqrt(jnp.sum(squares[...], axis=1, keepdims=True) / width + norm_eps)
        table = jnp.concatenate(load_rows(meta, slice(None)), axis=0)
        coef = gates_of(table, spot[0], ramp_step, top)
        pg = recip * acc_g[...]
        pu = recip * acc_u[...]
        pre_gate[...] = pg
        pre_up[...] = pu
        hidden[...] = (coef * (pg * jax.nn.sigmoid(pg) * pu)).astype(jnp.bfloat16)
        lane = lax.broadcasted_iota(jnp.int32, side.shape, 1)
        side[...] = jnp.where(lane == 0, recip, jnp.where(lane == 1, coef, 0.0))

    @pl.when(i >= steps)
    def _():
        out = matmul(hidden[...], wd[...]).astype(jnp.bfloat16)
        size = parts[0].shape[0]
        for p, ref in enumerate(parts):
            ref[...] = out[p * size : (p + 1) * size]


def backward_kernel(*refs, pieces, steps, width, torus):
    spot = refs[0]
    grad = refs[1 : 1 + pieces]
    tok = refs[1 + pieces : 1 + 2 * pieces]
    wd, wg, wu, pre_gate, pre_up, side = refs[1 + 2 * pieces : 7 + 2 * pieces]
    outs = refs[7 + 2 * pieces :]
    og_all, pre_grads = outs[:2]
    parts = outs[2:-4]
    acc, gate_s, up_s, gain_ref = outs[-4:]
    i = pl.program_id(0)
    size = parts[0].shape[0]

    @pl.when(i < steps)
    def _():
        for p, rows in enumerate(load_rows(grad, slice(None))):
            each = rows.shape[0]
            og_all[p * each : (p + 1) * each, :] = rows.astype(jnp.bfloat16)
        got = contract_cols(og_all[...], wd[...])

        @pl.when(i == 0)
        def _():
            acc[...] = got
            gain_ref[...] = jnp.zeros_like(gain_ref)

        @pl.when(i > 0)
        def _():
            acc[...] += got

    @pl.when(i == steps - 1)
    def _():
        recip = side[:, 0:1]
        coef = side[:, 1:2]
        pre_grads_of(acc, pre_gate, pre_up, recip, coef, gate_s, up_s, pre_grads)

    for k in range(steps):

        @pl.when(i == steps + k)
        def _(k=k):
            back = contract_cols(gate_s[...], wg[...]) + contract_cols(up_s[...], wu[...])
            recip = side[:, 0:1]
            total = None
            for p, x in enumerate(load_rows(tok, slice(None))):
                each = x.shape[0]
                rows = slice(p * each, (p + 1) * each)
                part = back[rows] * (x * recip[rows])
                total = part if p == 0 else total + part
            keep_gain(gain_ref, total, k * CHUNK // META)
            out = back.astype(jnp.bfloat16)
            for p, ref in enumerate(parts):
                ref[...] = out[p * size : (p + 1) * size]

    @pl.when(i == 2 * steps)
    def _():
        out = gain_block(torus, spot, gain_ref, width, side.shape[0])
        for p, ref in enumerate(parts):
            ref[:, :META] = out[p * size : (p + 1) * size]


def up_grads_kernel(scaled, pre_grads, wg_grad, wu_grad):
    both = contract_rows(scaled[...], pre_grads[...]).astype(jnp.bfloat16)
    half = wg_grad.shape[1]
    wg_grad[...] = both[:, :half]
    wu_grad[...] = both[:, half:]


def down_grad_kernel(hidden, og_all, wd_grad):
    wd_grad[...] = contract_rows(hidden[...], og_all[...]).astype(jnp.bfloat16)


def params(mib=56):
    return pltpu.CompilerParams(dimension_semantics=("arbitrary",), vmem_limit_bytes=mib * 2**20)


def placed(shapes):
    return [pltpu.VMEM(s.shape, s.dtype) for s in shapes]


def shapes_of(rows, width, hid, size, parts):
    scratch = [
        jax.ShapeDtypeStruct((rows, width), jnp.bfloat16),
        jax.ShapeDtypeStruct((rows, hid), jnp.float32),
        jax.ShapeDtypeStruct((rows, hid), jnp.float32),
        jax.ShapeDtypeStruct((rows, hid), jnp.bfloat16),
        jax.ShapeDtypeStruct((rows, META), jnp.float32),
    ]
    return scratch + [jax.ShapeDtypeStruct((size, width), jnp.bfloat16)] * parts


def limit(mib):
    return pltpu.CompilerParams(vmem_limit_bytes=mib * 2**20)


def cost(flops, size):
    return pl.CostEstimate(flops=int(flops), bytes_accessed=int(size), transcendentals=0)


def forward(torus, tok, gain, wg, wu, wd, spot, ramp_step, top):
    width, hid = wg.shape
    steps = width // CHUNK
    pieces = len(tok)
    heights = [t.shape[0] for t in tok]
    rows = sum(heights)
    n3 = torus.size(2)
    size = rows // (CORES * n3)
    first = lambda i: jnp.minimum(i, steps - 1)
    later = lambda i: jnp.maximum(i - steps, 0)
    fixed = lambda i: (0, 0)
    if rows <= WHOLE_ROWS:
        vmem = pl.BlockSpec(memory_space=pltpu.VMEM)
        shapes = shapes_of(rows, width, hid, size, CORES * n3)
        outs = pl.pallas_call(
            functools.partial(forward_whole, pieces=pieces, width=width, top=top),
            in_specs=[pl.BlockSpec(memory_space=pltpu.SMEM)] * 2 + [vmem] * (pieces + 3),
            out_specs=[pl.BlockSpec(memory_space=pltpu.HBM)] + [vmem] * 4,
            out_shape=[pltpu.HBM(shapes[0].shape, shapes[0].dtype)] + placed(shapes[1:5]),
            scratch_shapes=[
                pltpu.VMEM((rows, hid), jnp.float32),
                pltpu.VMEM((rows, hid), jnp.float32),
                pltpu.VMEM((rows, width), jnp.bfloat16),
                pltpu.SemaphoreType.DMA((width // WIDE,)),
            ],
            compiler_params=limit(12),
            cost_estimate=cost(4 * rows * width * hid, 4 * width * hid + 4 * rows * width),
            name="forward",
        )(spot, ramp_step, *tok, gain, *on_chip(wg, wu))
        parts = pl.pallas_call(
            out_whole,
            in_specs=[vmem] * 2,
            out_specs=[vmem] * (CORES * n3),
            out_shape=placed(shapes[5:]),
            compiler_params=limit(5),
            cost_estimate=cost(2 * rows * width * hid, 2 * width * hid + 2 * rows * width),
            name="out",
        )(*on_chip(outs[3], wd))
        return (*outs, [parts[c * n3 : (c + 1) * n3] for c in range(CORES)])
    outs = pl.pallas_call(
        functools.partial(forward_kernel, pieces=pieces, steps=steps, width=width, top=top),
        grid=(2 * steps,),
        in_specs=[pl.BlockSpec(memory_space=pltpu.SMEM)] * 2
        + [pl.BlockSpec((h, CHUNK), lambda i: (0, first(i))) for h in heights]
        + [pl.BlockSpec((h, META), lambda i: (0, width // META)) for h in heights]
        + [
            pl.BlockSpec((1, CHUNK), lambda i: (0, first(i))),
            pl.BlockSpec((CHUNK, hid), lambda i: (first(i), 0)),
            pl.BlockSpec((CHUNK, hid), lambda i: (first(i), 0)),
            pl.BlockSpec((hid, CHUNK), lambda i: (0, later(i))),
        ],
        out_specs=[
            pl.BlockSpec((rows, CHUNK), lambda i: (0, first(i))),
            pl.BlockSpec((rows, hid), fixed),
            pl.BlockSpec((rows, hid), fixed),
            pl.BlockSpec((rows, hid), fixed),
            pl.BlockSpec((rows, META), fixed),
        ]
        + [pl.BlockSpec((size, CHUNK), lambda i: (0, later(i)))] * (CORES * n3),
        out_shape=shapes_of(rows, width, hid, size, CORES * n3),
        scratch_shapes=[
            pltpu.VMEM((rows, hid), jnp.float32),
            pltpu.VMEM((rows, hid), jnp.float32),
            pltpu.VMEM((rows, META), jnp.float32),
        ],
        compiler_params=params(),
        cost_estimate=cost(6 * rows * width * hid, 6 * width * hid + 6 * rows * width),
        name="forward",
    )(spot, ramp_step, *tok, *tok, gain, wg, wu, wd)
    scaled, pre_gate, pre_up, hidden, side = outs[:5]
    parts = [outs[5 + c * n3 : 5 + (c + 1) * n3] for c in range(CORES)]
    return scaled, pre_gate, pre_up, hidden, side, parts


def backward(torus, spot, grad, tok, wd, wg, wu, pre_gate, pre_up, side):
    width, hid = wg.shape
    steps = width // CHUNK
    pieces = len(grad)
    heights = [g.shape[0] for g in grad]
    rows = sum(heights)
    n3 = torus.size(2)
    size = rows // (CORES * n3)
    first = lambda i: jnp.minimum(i, steps - 1)
    later = lambda i: jnp.maximum(i - steps, 0)
    held = lambda i: jnp.clip(i - steps, 0, steps - 1)
    fixed = lambda i: (0, 0)
    shapes = [
        jax.ShapeDtypeStruct((rows, width), jnp.bfloat16),
        jax.ShapeDtypeStruct((rows, 2 * hid), jnp.bfloat16),
    ] + [jax.ShapeDtypeStruct((size, width + META), jnp.bfloat16)] * (CORES * n3)
    if rows <= WHOLE_ROWS:
        vmem = pl.BlockSpec(memory_space=pltpu.VMEM)
        outs = pl.pallas_call(
            functools.partial(backward_whole, pieces=pieces, width=width, torus=torus),
            in_specs=[pl.BlockSpec(memory_space=pltpu.SMEM)]
            + [vmem] * (2 * pieces)
            + [pl.BlockSpec(memory_space=pltpu.HBM)]
            + [vmem] * 5,
            out_specs=[vmem] * (2 + CORES * n3),
            out_shape=placed(shapes),
            scratch_shapes=[
                pltpu.VMEM((rows, hid), jnp.float32),
                pltpu.VMEM((rows, hid), jnp.bfloat16),
                pltpu.VMEM((rows, hid), jnp.bfloat16),
                pltpu.VMEM((width // META + 8, META), jnp.float32),
                pltpu.VMEM((hid, width), jnp.bfloat16),
                pltpu.SemaphoreType.DMA((width // WIDE,)),
            ],
            compiler_params=limit(17),
            cost_estimate=cost(6 * rows * width * hid, 6 * width * hid + 6 * rows * width),
            name="backward",
        )(spot, *grad, *tok, *off_chip(wd), *on_chip(wg, wu, pre_gate, pre_up, side))
        return (*outs[:2], [outs[2 + c * n3 : 2 + (c + 1) * n3] for c in range(CORES)])
    outs = pl.pallas_call(
        functools.partial(backward_kernel, pieces=pieces, steps=steps, width=width, torus=torus),
        grid=(2 * steps + 1,),
        in_specs=[pl.BlockSpec(memory_space=pltpu.SMEM)]
        + [pl.BlockSpec((h, CHUNK), lambda i: (0, first(i))) for h in heights]
        + [pl.BlockSpec((h, CHUNK), lambda i: (0, held(i))) for h in heights]
        + [
            pl.BlockSpec((hid, CHUNK), lambda i: (0, first(i))),
            pl.BlockSpec((CHUNK, hid), lambda i: (held(i), 0)),
            pl.BlockSpec((CHUNK, hid), lambda i: (held(i), 0)),
            pl.BlockSpec((rows, hid), fixed),
            pl.BlockSpec((rows, hid), fixed),
            pl.BlockSpec((rows, META), fixed),
        ],
        out_specs=[
            pl.BlockSpec((rows, CHUNK), lambda i: (0, first(i))),
            pl.BlockSpec((rows, 2 * hid), fixed),
        ]
        + [pl.BlockSpec((size, CHUNK), lambda i: (0, later(i)))] * (CORES * n3),
        out_shape=shapes,
        scratch_shapes=[
            pltpu.VMEM((rows, hid), jnp.float32),
            pltpu.VMEM((rows, hid), jnp.bfloat16),
            pltpu.VMEM((rows, hid), jnp.bfloat16),
            pltpu.VMEM((width // META + 8, META), jnp.float32),
        ],
        compiler_params=params(),
        cost_estimate=cost(6 * rows * width * hid, 6 * width * hid + 6 * rows * width),
        name="backward",
    )(spot, *grad, *tok, wd, wg, wu, pre_gate, pre_up, side)
    parts = [outs[2 + c * n3 : 2 + (c + 1) * n3] for c in range(CORES)]
    return outs[0], outs[1], parts


def up_grads(scaled, pre_grads):
    rows, width = scaled.shape
    hid = pre_grads.shape[1] // 2
    step = WIDE if rows <= WHOLE_ROWS else CHUNK
    return pl.pallas_call(
        up_grads_kernel,
        grid=(width // step,),
        in_specs=[
            pl.BlockSpec((rows, step), lambda i: (0, i)),
            pl.BlockSpec((rows, 2 * hid), lambda i: (0, 0)),
        ],
        out_specs=[pl.BlockSpec((step, hid), lambda i: (i, 0))] * 2,
        out_shape=[jax.ShapeDtypeStruct((width, hid), jnp.bfloat16)] * 2,
        compiler_params=params(20),
        cost_estimate=cost(4 * rows * width * hid, 4 * width * hid + 2 * rows * width),
        name="up_grads",
    )(scaled, pre_grads)


def down_grad(hidden, og_all):
    rows, width = og_all.shape
    hid = hidden.shape[1]
    step = WIDE if rows <= WHOLE_ROWS else CHUNK
    return pl.pallas_call(
        down_grad_kernel,
        grid=(width // step,),
        in_specs=[
            pl.BlockSpec((rows, hid), lambda i: (0, 0)),
            pl.BlockSpec((rows, step), lambda i: (0, i)),
        ],
        out_specs=pl.BlockSpec((hid, step), lambda i: (0, i)),
        out_shape=jax.ShapeDtypeStruct((hid, width), jnp.bfloat16),
        compiler_params=params(20),
        cost_estimate=cost(2 * rows * width * hid, 2 * width * hid + 2 * rows * width),
        name="down_grad",
    )(*(on_chip(hidden, og_all) if rows <= WHOLE_ROWS else (hidden, og_all)))


def layer(tokens, out_grad, routes, gate_fixed, ramp_step, norm_gain, w_gate, w_up, w_down):
    seq_count = lax.axis_size("seq")
    ep_count = lax.axis_size("ep")
    torus = Torus(seq_count, ep_count)
    torus.check()
    width = tokens.shape[1]
    top = routes.shape[1]
    tok = gather(torus, pack(tokens, routes, gate_fixed))
    grad = gather(torus, out_grad)
    expert = lax.axis_index("ep")
    span = width // torus.count
    device = lax.axis_index("seq") * ep_count + expert
    start = (device * span % META).astype(jnp.uint32)
    spot = jnp.stack([expert.astype(jnp.uint32), device.astype(jnp.uint32), start])
    gain = norm_gain[None, :]
    wg, wu, wd = w_gate[0], w_up[0], w_down[0]
    if tokens.shape[0] * seq_count * ep_count <= WHOLE_ROWS:
        held = []
        for weight in (wg, wu):
            held += prefetch(spot, [weight])
        wg, wu = held
    scaled, pre_gate, pre_up, hidden, side, out_parts = forward(
        torus, tok, gain, wg, wu, wd, spot, ramp_step, top
    )
    og_all, pre_grads, parts = backward(torus, spot, grad, tok, wd, wg, wu, pre_gate, pre_up, side)
    w_gate_grad, w_up_grad = up_grads(scaled, pre_grads)
    w_down_grad = down_grad(hidden, og_all)
    mixed, w_gate_grad = scatter_sum(torus, out_parts, w_gate_grad)
    mixed = mixed.astype(jnp.bfloat16)
    total = scatter_sum(torus, parts)
    normed_grad = total[:, :width]
    count = gain_rows(span)
    gain_part = total[:count, width:] + total[count : 2 * count, width:]
    gain_grad = lax.dynamic_slice(gain_part.reshape(-1), (start,), (span,))
    own = tokens.astype(jnp.float32)
    own_recip = lax.rsqrt(jnp.mean(own * own, axis=1, keepdims=True) + norm_eps)
    weighted = gain * normed_grad
    inner = jnp.sum(weighted * own, axis=1, keepdims=True)
    tokens_grad = (
        own_recip * weighted - own * own_recip * own_recip * own_recip * inner / width
    ).astype(jnp.bfloat16)
    return (mixed, tokens_grad, gain_grad, w_gate_grad[None], w_up_grad[None], w_down_grad[None])


def solution(mesh):
    return jax.shard_map(
        layer,
        mesh=mesh,
        in_specs=(
            P(("seq", "ep"), None),
            P(("seq", "ep"), None),
            P(("seq", "ep"), None),
            P(("seq", "ep"), None),
            P(),
            P(),
            P("ep", None, "seq"),
            P("ep", None, "seq"),
            P("ep", "seq", None),
        ),
        out_specs=(
            P(("seq", "ep"), None),
            P(("seq", "ep"), None),
            P(("seq", "ep")),
            P("ep", None, "seq"),
            P("ep", None, "seq"),
            P("ep", "seq", None),
        ),
        check_vma=False,
    )
```
